256 devices in a mesh: row: 16 (over y_hi, z), col: 16 (over y_lo, x, core).
Axes of the slice: x: 4, y: 4 (y_hi: 2, y_lo: 2; y = y_hi * 2 + y_lo), z: 8, core: 2. Of those that a mesh axis runs over, the one named last changes fastest.
Arguments:
- x_tiles: bfloat16 [256, 2048, 128], P('row', 'col'), may hold values from -1.328125 to 1.328125
- tile_pos: int32 [16, 256], P('row', 'col'), may hold values from 0 to 63, as said below
- panel_ids: int32 [4], replicated, may hold values from 0 to 31, as said below
Outputs:
- square_part: float32 [16384, 16384], P('row', 'col')
The draws below stay inside these ranges and needn't reach their ends.
Inputs may be any that keep to these rules, and one draw needn't show every extreme that they name: `tile_pos`: on each device the 16 positions are distinct and increasing. Split the device's 8 x 8 local blocks into squares of 4 x 4 blocks aligned to multiples of 4: one square (drawn) holds exactly 10 stored blocks and every other square exactly 2. `panel_ids`: the 4 panels are distinct, and one of them is the last panel.
All inputs are finite; a program needn't handle non-finite values.
Results may differ from the reference program's by a relative error of at most 0.0003.
Values may be sent and summed in bfloat16 or wider, within the bound.
A program may use at most 64 MiB of HBM per device.

```python
import jax
import jax.numpy as jnp

BS = 128
LR = 8
PW = 4
SECTIONS = 4
QD = 10
QS = 2
NB = 128
LC = 8
SLOTS = 16
N_ROW = 16
N_COL = 16


def draw_tile_pos(key, part):
    qrows = LR // PW
    qcols = LC // PW
    squares = qrows * qcols
    cells = PW * PW

    def one_device(device):
        dev_key = jax.random.fold_in(jax.random.fold_in(key, 7001), device)
        key_win, key_perm = jax.random.split(dev_key)
        winner = jax.random.randint(key_win, (), 0, squares)
        index = jnp.arange(squares, dtype=jnp.int32)
        counts = jnp.where(index == winner, QD, QS).astype(jnp.int32)
        ranks = jax.vmap(lambda sub: jax.random.permutation(sub, cells))(jax.random.split(key_perm, squares))
        chosen = (ranks < counts[:, None]).reshape(qrows, qcols, PW, PW)
        chosen = chosen.transpose(0, 2, 1, 3).reshape(-1)
        return jnp.nonzero(chosen, size=SLOTS)[0].astype(jnp.int32)
    all_rows = jax.vmap(one_device)(jnp.arange(N_ROW * N_COL, dtype=jnp.int32))
    return all_rows.reshape(N_ROW, N_COL * SLOTS).astype(jnp.int32)


def draw_panel_ids(key, part):
    panels = NB // PW
    others = jax.random.permutation(jax.random.fold_in(key, 9103), panels - 1)[:SECTIONS - 1].astype(jnp.int32)
    picked = jnp.concatenate([others, jnp.full((1,), panels - 1, jnp.int32)])
    order = jax.random.permutation(jax.random.fold_in(key, 9107), SECTIONS)
    return picked[order].astype(jnp.int32)


def steps_of(own_key, dims, pieces, least, largest):
    factor_of = 1.0
    for axis_at, blocks in pieces:
        draws = jax.random.uniform(jax.random.fold_in(jax.random.fold_in(own_key, 6), axis_at), (blocks,), jnp.float32, least / len(pieces), largest / len(pieces))
        factor_of = factor_of * jnp.repeat(jnp.exp(draws), dims[axis_at] // blocks).reshape((-1,) + (1,) * (len(dims) - 1 - axis_at))
    return factor_of


def scatter_about(key, shape, spread, most, shards=(), kind=jnp.bfloat16):
    result = spread * jax.random.normal(key, shape, jnp.float32)
    if shards:
        result = result * steps_of(key, shape, shards, -0.22, 0.18)
    return jnp.clip(result, -most, most).astype(kind)


def setup_inputs(seed: int = 0) -> dict:
    streams_of = jax.random.split(jax.random.key(seed), 4)
    return {
        "x_tiles": scatter_about(streams_of[0], (N_ROW * SLOTS, N_COL * BS, BS), ((SECTIONS * PW * BS // 5) ** -0.25), 1.328125, ((0, 16), (1, 16))),
        "tile_pos": draw_tile_pos(jax.random.fold_in(streams_of[3], 71), 0),
        "panel_ids": draw_panel_ids(jax.random.fold_in(streams_of[3], 71), 0),
    }


def reference(x_tiles, tile_pos, panel_ids):
    tiles = x_tiles.reshape(N_ROW, SLOTS, N_COL, BS, BS).transpose(0, 2, 1, 3, 4).reshape(N_ROW * N_COL * SLOTS, BS, BS)
    positions = tile_pos.reshape(N_ROW, N_COL, SLOTS)
    row_base = (jnp.arange(N_ROW, dtype=jnp.int32) * LR)[:, None, None]
    col_base = (jnp.arange(N_COL, dtype=jnp.int32) * LC)[None, :, None]
    glob_rows = (row_base + positions // LC).reshape(-1).astype(jnp.int32)
    glob_cols = (col_base + positions % LC).reshape(-1).astype(jnp.int32)
    square_part = jnp.zeros((NB * BS, NB * BS), jnp.float32)
    for section in range(SECTIONS):
        first = (panel_ids[section] * PW).astype(jnp.int32)
        col_rel = glob_cols - first
        col_in = (col_rel >= 0) & (col_rel < PW)
        col_idx = jnp.where(col_in, col_rel, PW).astype(jnp.int32)
        column_blocks = jnp.zeros((NB, PW, BS, BS), x_tiles.dtype).at[glob_rows, col_idx].set(tiles, mode="drop")
        column_panel = column_blocks.transpose(0, 2, 1, 3).reshape(NB * BS, PW * BS)
        row_rel = glob_rows - first
        row_in = (row_rel >= 0) & (row_rel < PW)
        row_idx = jnp.where(row_in, row_rel, PW).astype(jnp.int32)
        row_blocks = jnp.zeros((PW, NB, BS, BS), x_tiles.dtype).at[row_idx, glob_cols].set(tiles, mode="drop")
        row_panel = row_blocks.transpose(0, 2, 1, 3).reshape(PW * BS, NB * BS)
        square_part = square_part + jnp.dot(column_panel, row_panel, preferred_element_type=jnp.float32)
    return square_part
```

```python
import functools

import jax
import jax.numpy as jnp
from jax import lax
from jax.experimental import pallas as pl
from jax.experimental.pallas import tpu as pltpu
from jax.sharding import PartitionSpec as P

BS = 128
LR = 8
LC = 8
PW = 4
SECTIONS = 4
SLOTS = 16
WIN = 12
HALF_WIN = WIN // 2
LOW = SLOTS - WIN
CH = 32
NZ, NX = 8, 4
MB, MA = 2, 1
NB_R = HALF_WIN * (BS // CH)
NA_R = HALF_WIN * (BS // 2 // CH)
SB_R = NB_R + (NZ - 1) * MB
TB_R = SB_R - MB
SA_R = NA_R + (NX - 1) * MA
TA_R = SA_R - MA
MESH = pl.DeviceIdType.MESH

NEEDED = []
for _i in range(HALF_WIN):
    _all = [_i, _i + LOW, _i + HALF_WIN, _i + HALF_WIN + LOW]
    NEEDED.append([s for s in _all if all(s not in prev for prev in NEEDED)])


def sort_kernel(pos, x_ref, o_ref):
    def count(s, n):
        return n + jnp.where((pos[0, s] % LC) < PW, 1, 0)

    left = lax.fori_loop(0, SLOTS, count, 0)

    def place(s, carry):
        a, b = carry
        is_left = (pos[0, s] % LC) < PW
        o_ref[jnp.where(is_left, a, b)] = x_ref[s]
        one = jnp.where(is_left, 1, 0)
        return a + one, b + 1 - one

    lax.fori_loop(0, SLOTS, place, (0, left))


def comm_kernel(
    panels, x_ref, xa_ref, sb, sa, sx,
    pb, pa, rb, ra,
    xb_send, xa_send, xb_recv, xa_recv,
    b_send, b_recv, a_send, a_recv, s_send, s_recv,
):
    row = lax.axis_index("row")
    col = lax.axis_index("col")
    core = lax.rem(col, 2)
    z, yh = lax.rem(row, NZ), row // NZ
    x, yl = lax.rem(col // 2, NX), col // 8

    def rowdev(zz, yy):
        return {"row": yy * NZ + zz, "col": col}

    def coldev(xx, yy, cc):
        return {"row": row, "col": (yy * NX + xx) * 2 + cc}

    z_to = [rowdev(lax.rem(z + 1, NZ), yh), rowdev(lax.rem(z + NZ - 1, NZ), yh)]
    x_to = [coldev(lax.rem(x + 1, NX), yl, core), coldev(lax.rem(x + NX - 1, NX), yl, core)]
    y_row = rowdev(z, 1 - yh)
    sibling = coldev(x, yl, 1 - core)
    y_col = coldev(x, 1 - yl, core)
    diag = coldev(x, 1 - yl, 1 - core)

    barrier = pltpu.get_barrier_semaphore()
    peers = z_to + x_to + [y_row, sibling, y_col, diag]
    for dev in peers:
        pl.semaphore_signal(barrier, inc=1, device_id=dev, device_id_type=MESH)
    pl.semaphore_wait(barrier, len(peers))

    mine = pl.ds(pl.multiple_of(core * 64, 64), 64)
    other = pl.ds(pl.multiple_of((1 - core) * 64, 64), 64)

    def b_hand(s):
        return pltpu.make_async_remote_copy(
            src_ref=x_ref.at[s], dst_ref=pb.at[s], send_sem=xb_send, recv_sem=xb_recv.at[s],
            device_id=y_row, device_id_type=MESH)

    def a_hand(j, s):
        dev, rows = [(sibling, other), (y_col, mine), (diag, other)][j]
        return pltpu.make_async_remote_copy(
            src_ref=xa_ref.at[s, rows], dst_ref=pa.at[j, s], send_sem=xa_send.at[j],
            recv_sem=xa_recv.at[j, s], device_id=dev, device_id_type=MESH)

    for slots in NEEDED:
        for s in slots:
            b_hand(s).start()
            for j in range(3):
                a_hand(j, s).start()

    def b_copy(d, t):
        return pltpu.make_async_remote_copy(
            src_ref=sb.at[d, t], dst_ref=rb.at[d, t], send_sem=b_send.at[d],
            recv_sem=b_recv.at[d, t], device_id=z_to[d], device_id_type=MESH)

    def a_copy(d, t):
        return pltpu.make_async_remote_copy(
            src_ref=sa.at[d, t], dst_ref=ra.at[d, t], send_sem=a_send.at[d],
            recv_sem=a_recv.at[d, t], device_id=x_to[d], device_id_type=MESH)

    def s_copy(d, t):
        return pltpu.make_async_remote_copy(
            src_ref=sa.at[d, t], dst_ref=sx.at[d, t], send_sem=s_send.at[d],
            recv_sem=s_recv.at[d], device_id=sibling, device_id_type=MESH)

    owner = [panels[k] // 2 for k in range(SECTIONS)]
    high = [panels[k] % 2 == 1 for k in range(SECTIONS)]
    b_own = [owner[k] == row for k in range(SECTIONS)]
    b_oth = [owner[k] == (1 - yh) * NZ + z for k in range(SECTIONS)]

    def at(cc, yy):
        return [owner[k] == (yy * NX + x) * 2 + cc for k in range(SECTIONS)]

    a_own = at(core, yl)
    a_oth = [at(1 - core, yl), at(core, 1 - yl), at(1 - core, 1 - yl)]

    def b_round(t, i, q, first):
        rows = pl.ds(q * CH, CH)
        for d in range(2):
            s0 = i + HALF_WIN * d
            if not first:
                b_copy(d, t - MB).wait_recv()
            own = x_ref[s0, rows, :], x_ref[s0 + LOW, rows, :]
            oth = pb[s0, rows, :], pb[s0 + LOW, rows, :]
            for k in range(SECTIONS):
                v = lax.select(high[k], oth[1], oth[0])
                if not first:
                    v = lax.select(b_oth[k], v, rb[d, t - MB, k])
                v = lax.select(b_own[k], lax.select(high[k], own[1], own[0]), v)
                sb[d, t, k] = v
            b_copy(d, t).start()

    def a_round(t, i, q, first):
        rows = pl.ds(q * CH, CH)
        own_rows = pl.ds(pl.multiple_of(core * 64 + q * CH, CH), CH)
        for d in range(2):
            s0 = i + HALF_WIN * d
            if not first:
                a_copy(d, t - MA).wait_recv()
            own = xa_ref[s0, own_rows, :], xa_ref[s0 + LOW, own_rows, :]
            oth = [(pa[j, s0, rows, :], pa[j, s0 + LOW, rows, :]) for j in range(3)]
            for k in range(SECTIONS):
                v = own[0] if first else ra[d, t - MA, k]
                v = lax.select(a_own[k], lax.select(high[k], own[1], own[0]), v)
                for j in range(3):
                    v = lax.select(a_oth[j][k], lax.select(high[k], oth[j][1], oth[j][0]), v)
                sa[d, t, k] = v
            a_copy(d, t).start()
            s_copy(d, t).start()

    for i in range(HALF_WIN):
        for s in NEEDED[i]:
            b_hand(s).wait_recv()
            for j in range(3):
                a_hand(j, s).wait_recv()

        def pair(h, _, i=i):
            a_round(2 * i + h, i, h, False)
            b_round(4 * i + 2 * h, i, 2 * h, False)
            b_round(4 * i + 2 * h + 1, i, 2 * h + 1, False)
            return 0

        if i == 0:
            for t in range(4):
                if t % 2 == 0:
                    a_round(t // 2, 0, t // 2, t // 2 < MA)
                b_round(t, 0, t, t < MB)
        else:
            lax.fori_loop(0, 2, pair, 0)

    def a_tail(t, _):
        for d in range(2):
            a_copy(d, t - MA).wait_recv()
            sa[d, t] = ra[d, t - MA]
            @pl.when(t < TA_R)
            def _():
                a_copy(d, t).start()
            s_copy(d, t).start()
        return 0

    def b_tail(t, _):
        for d in range(2):
            b_copy(d, t - MB).wait_recv()
            sb[d, t] = rb[d, t - MB]
            @pl.when(t < TB_R)
            def _():
                b_copy(d, t).start()
        return 0

    def both_tail(j, _):
        a_tail(NA_R + j, 0)
        for u in range(2):
            b_tail(NB_R + 2 * j + u, 0)
        return 0

    joint = SA_R - NA_R
    lax.fori_loop(0, joint, both_tail, 0)
    lax.fori_loop(NB_R + 2 * joint, SB_R, b_tail, 0)

    pltpu.make_async_copy(x_ref, x_ref, xb_send).wait()
    for j in range(3):
        pltpu.make_async_copy(pa.at[j], pa.at[j], xa_send.at[j]).wait()
    for d in range(2):
        sent = sb.at[d, pl.ds(0, TB_R)]
        pltpu.make_async_copy(sent, sent, b_send.at[d]).wait()
        sent = sa.at[d, pl.ds(0, TA_R)]
        pltpu.make_async_copy(sent, sent, a_send.at[d]).wait()
        pltpu.make_async_copy(sa.at[d], sa.at[d], s_send.at[d]).wait()
        pltpu.make_async_copy(sx.at[d], sx.at[d], s_recv.at[d]).wait()


def product_kernel(panels, pos_a, pos_b, where_am_i, sb, sa, sx, c_ref, a_full, b_full):
    @pl.when(pl.program_id(0) == 0)
    def _():
        row, col = where_am_i[0], where_am_i[1]
        z, x, core = row % NZ, (col // 2) % NX, col % 2
        a_full[...] = jnp.zeros_like(a_full)
        b_full[...] = jnp.zeros_like(b_full)

        def section(k, _):
            panel = panels[k]
            owner = panel // 2
            high = panel % 2
            zo, xo = owner % NZ, (owner // 2) % NX
            db = [(z - zo + NZ) % NZ, (zo - z + NZ) % NZ]
            da = [(x - xo + NX) % NX, (xo - x + NX) % NX]

            def left(s, n):
                return n + jnp.where((pos_a[owner, s] % LC) < PW, 1, 0)

            skip = jnp.where(high == 1, lax.fori_loop(0, SLOTS, left, 0) - LOW, 0)

            def tile(s, w):
                p = pos_b[owner, s]
                @pl.when((p // LC) // PW == high)
                def _():
                    wb = s - LOW * high
                    d = wb // HALF_WIN
                    t = jnp.where(d == 0, db[0], db[1]) * MB + (wb % HALF_WIN) * (BS // CH)
                    kk = (p // LC) % PW
                    r0 = pl.multiple_of((k * PW + kk) * BS, BS)
                    c0 = pl.multiple_of((p % LC) * BS, BS)
                    v = sb[d, pl.ds(t, BS // CH), k].reshape(BS, BS)
                    b_full[pl.ds(r0, BS), pl.ds(c0, BS)] = v
                p = pos_a[owner, s]
                hit = (p % LC) // PW == high
                @pl.when(hit)
                def _():
                    d = w // HALF_WIN
                    t = jnp.where(d == 0, da[0], da[1]) * MA + (w % HALF_WIN) * (BS // 2 // CH)
                    kk = (p % LC) % PW
                    r0 = pl.multiple_of((p // LC) * BS, BS)
                    c0 = pl.multiple_of((k * PW + kk) * BS, BS)
                    ours = sa[d, pl.ds(t, BS // 2 // CH), k].reshape(BS // 2, BS)
                    theirs = sx[d, pl.ds(t, BS // 2 // CH), k].reshape(BS // 2, BS)
                    r1 = pl.multiple_of(r0 + core * 64, 64)
                    r2 = pl.multiple_of(r0 + (1 - core) * 64, 64)
                    a_full[pl.ds(r1, BS // 2), pl.ds(c0, BS)] = ours
                    a_full[pl.ds(r2, BS // 2), pl.ds(c0, BS)] = theirs
                return w + jnp.where(hit, 1, 0)

            lax.fori_loop(0, SLOTS, tile, skip)
            return 0

        lax.fori_loop(0, SECTIONS, section, 0)

    rows = c_ref.shape[0]
    r0 = pl.multiple_of(pl.program_id(0) * rows, rows)
    c_ref[...] = jnp.dot(
        a_full[pl.ds(r0, rows), :], b_full[...], preferred_element_type=jnp.float32)


def per_device(x_tiles, tile_pos, panel_ids):
    vmem = pl.BlockSpec(memory_space=pltpu.VMEM)
    smem = pl.BlockSpec(memory_space=pltpu.SMEM)
    bf16 = jnp.bfloat16
    pos_a = lax.all_gather(tile_pos[0], "col")
    pos_b = lax.all_gather(tile_pos[0], "row")
    xa = pl.pallas_call(
        sort_kernel,
        out_shape=jax.ShapeDtypeStruct((SLOTS, BS, BS), bf16),
        in_specs=[smem, vmem],
        out_specs=vmem,
        name="sort_slots",
    )(tile_pos, x_tiles)
    dma = pltpu.SemaphoreType.DMA
    sb, sa, sx = pl.pallas_call(
        comm_kernel,
        out_shape=[
            jax.ShapeDtypeStruct((2, SB_R, SECTIONS, CH, BS), bf16),
            jax.ShapeDtypeStruct((2, SA_R, SECTIONS, CH, BS), bf16),
            jax.ShapeDtypeStruct((2, SA_R, SECTIONS, CH, BS), bf16),
        ],
        in_specs=[smem, vmem, vmem],
        out_specs=[vmem, vmem, vmem],
        scratch_shapes=[
            pltpu.VMEM((SLOTS, BS, BS), bf16),
            pltpu.VMEM((3, SLOTS, BS // 2, BS), bf16),
            pltpu.VMEM((2, TB_R, SECTIONS, CH, BS), bf16),
            pltpu.VMEM((2, TA_R, SECTIONS, CH, BS), bf16),
            dma, dma((3,)), dma((SLOTS,)), dma((3, SLOTS)),
            dma((2,)), dma((2, TB_R)), dma((2,)), dma((2, TA_R)), dma((2,)), dma((2,)),
        ],
        compiler_params=pltpu.CompilerParams(
            collective_id=0, has_side_effects=True, vmem_limit_bytes=40 << 20),
        name="spread_tiles",
    )(panel_ids, x_tiles, xa)
    here = jnp.stack([lax.axis_index("row"), lax.axis_index("col")]).astype(jnp.int32)
    n = LR * BS
    kdim = SECTIONS * PW * BS
    steps = 4
    return pl.pallas_call(
        product_kernel,
        out_shape=jax.ShapeDtypeStruct((n, LC * BS), jnp.float32),
        grid=(steps,),
        in_specs=[smem, smem, smem, smem, vmem, vmem, vmem],
        out_specs=pl.BlockSpec((n // steps, LC * BS), lambda i: (i, 0)),
        scratch_shapes=[pltpu.VMEM((n, kdim), bf16), pltpu.VMEM((kdim, LC * BS), bf16)],
        compiler_params=pltpu.CompilerParams(vmem_limit_bytes=48 << 20),
        cost_estimate=pl.CostEstimate(
            flops=2 * n * kdim * LC * BS, bytes_accessed=10 << 20, transcendentals=0),
        name="panel_product",
    )(panel_ids, pos_a, pos_b, here, sb, sa, sx)


def solution(mesh):
    in_specs = (P("row", "col", None), P("row", "col"), P())
    out_specs = P("row", "col")
    return jax.shard_map(
        per_device, mesh=mesh, in_specs=in_specs, out_specs=out_specs, check_vma=False
    )
```

```python
import jax
import jax.numpy as jnp
from jax import lax
from jax.experimental import pallas as pl
from jax.experimental.pallas import tpu as pltpu
from jax.sharding import PartitionSpec as P

BS = 128
LR = 8
LC = 8
PW = 4
SECTIONS = 4
SLOTS = 16
WIN = 12
HALF = WIN // 2
LOW = SLOTS - WIN
NZ, NX = 8, 4
CB, CA = 32, 64
MB, MA = 4, 4
QB, QA = BS // CB, BS // CA
NB_R, NA_R = HALF * QB, HALF * QA
TB_R, TA_R = NB_R + (NZ - 2) * MB, NA_R + (NX - 2) * MA
SB_R, SA_R = TB_R + MB, TA_R + MA
MESH = pl.DeviceIdType.MESH

NEEDED = []
for _i in range(HALF):
    _all = [_i, _i + LOW, _i + HALF, _i + HALF + LOW]
    NEEDED.append([s for s in _all if all(s not in prev for prev in NEEDED)])


def comm_kernel(
    panels, pos, x_hbm, sb, sa, meta,
    xv, xa, pc, rb, ra, mo, mc, mb, ma, mt,
    x_sem, h_send, h_recv, b_send, b_recv, a_send, a_recv, s_send, s_recv,
    mh_send, mh_recv, mr_send, mr_recv, mf_send, mf_recv,
):
    row = lax.axis_index("row")
    col = lax.axis_index("col")
    core = lax.rem(col, 2)
    z, yh = lax.rem(row, NZ), row // NZ
    x, yl = lax.rem(col // 2, NX), col // 8

    def dev(zz, yyh, xx, yyl, cc):
        return {"row": yyh * NZ + zz, "col": (yyl * NX + xx) * 2 + cc}

    z_to = [dev(lax.rem(z + 1, NZ), yh, x, yl, core), dev(lax.rem(z + NZ - 1, NZ), yh, x, yl, core)]
    x_to = [dev(z, yh, lax.rem(x + 1, NX), yl, core), dev(z, yh, lax.rem(x + NX - 1, NX), yl, core)]
    sibling = dev(z, yh, x, yl, 1 - core)
    yh_same, yh_cross = dev(z, 1 - yh, x, yl, core), dev(z, 1 - yh, x, yl, 1 - core)
    yl_same, yl_cross = dev(z, yh, x, 1 - yl, core), dev(z, yh, x, 1 - yl, 1 - core)

    def remote(src, dst, send, recv, to):
        return pltpu.make_async_remote_copy(
            src_ref=src, dst_ref=dst, send_sem=send, recv_sem=recv,
            device_id=to, device_id_type=MESH)

    local = pltpu.make_async_copy(x_hbm, xv, x_sem)
    local.start()
    barrier = pltpu.get_barrier_semaphore()

    def greet(peers):
        for peer in peers:
            pl.semaphore_signal(barrier, inc=1, device_id=peer, device_id_type=MESH)
        pl.semaphore_wait(barrier, len(peers))

    lane = lax.broadcasted_iota(jnp.int32, (8, BS), 1)
    where = jnp.zeros((8, BS), jnp.int32)
    spot = [pos[0, s] for s in range(SLOTS)]
    for s in range(SLOTS):
        where = jnp.where(lane == s, spot[s], where)
    mo[...] = where
    right = [lax.rem(p, LC) // PW for p in spot]
    n_left = SLOTS - sum(right)
    lefts, rights, rank = 0, n_left, []
    for s in range(SLOTS):
        rank.append(jnp.where(right[s] == 0, lefts, rights))
        lefts, rights = lefts + 1 - right[s], rights + right[s]
    local.wait()
    for i in range(SLOTS):
        src = sum(jnp.where(rank[s] == i, s, 0) for s in range(SLOTS))
        xa[i] = xv[src]

    owner = [panels[k] // 2 for k in range(SECTIONS)]
    high = [lax.rem(panels[k], 2) == 1 for k in range(SECTIONS)]

    def hand(source, to, j, s):
        return remote(source.at[s], pc.at[j, s], h_send.at[j], h_recv.at[j, s], to)

    def hand_meta(to, j):
        return remote(mo, mc.at[j], mh_send.at[j], mh_recv.at[j], to)

    def hand_over(plan):
        for _, to, j in plan:
            hand_meta(to, j).start()
        for slots in NEEDED:
            for s in slots:
                for source, to, j in plan:
                    hand(source, to, j, s).start()

    def handed(i):
        for s in NEEDED[i]:
            for j in range(3):
                hand(xv, sibling, j, s).wait_recv()

    def handed_meta():
        for j in range(3):
            hand_meta(sibling, j).wait_recv()

    def all_left(ref, sem):
        pltpu.make_async_copy(ref, ref, sem).wait()

    def pick(own, low_high, cond, v):
        return lax.select(cond, lax.select(own, low_high[1], low_high[0]), v)

    def b_copy(d, t):
        return remote(sb.at[d, t], rb.at[d, t], b_send.at[d], b_recv.at[d, t], z_to[d])

    def b_share(d, t):
        return remote(sb.at[d, t, 0], sb.at[d, t, 0], s_send.at[d], s_recv.at[d], sibling)

    def b_meta(j):
        return remote(mb.at[j], mb.at[j + 1], mr_send, mr_recv.at[j], z_to[0])

    @pl.when(core == 1)
    def _():
        greet(z_to + [sibling, yh_same, yh_cross, yl_cross])
        hand_over([(xa, sibling, 0), (xv, yh_same, 1), (xa, yl_cross, 2)])
        own_here = [owner[k] == row for k in range(SECTIONS)]
        own_there = [owner[k] == (1 - yh) * NZ + z for k in range(SECTIONS)]

        def b_round(t, i, q, first):
            rows = pl.ds(q * CB, CB)
            for d in range(2):
                s0 = i + HALF * d
                if not first:
                    b_copy(d, t - MB).wait_recv()
                for cc in range(2):
                    if cc == 1:
                        here = xv[s0, rows, :], xv[s0 + LOW, rows, :]
                    else:
                        here = pc[0, s0, rows, :], pc[0, s0 + LOW, rows, :]
                    j = 2 - cc
                    there = pc[j, s0, rows, :], pc[j, s0 + LOW, rows, :]
                    for k in range(SECTIONS):
                        v = here[0] if first else rb[d, t - MB, cc, k]
                        v = pick(high[k], there, own_there[k], v)
                        v = pick(high[k], here, own_here[k], v)
                        sb[d, t, cc, k] = v
                b_copy(d, t).start()
                b_share(d, t).start()

        for i in range(HALF):
            handed(i)
            if i == 0:
                handed_meta()
                for cc in range(2):
                    here = mo[0:1, :] if cc == 1 else mc[0, 0:1, :]
                    there = mc[2 - cc, 0:1, :]
                    for k in range(SECTIONS):
                        r = cc * SECTIONS + k
                        mb[0, r : r + 1, :] = jnp.where(own_here[k], here, there)
            else:
                b_meta(i - 1).wait_recv()
            b_meta(i).start()
            if i * QB < MB:
                for q in range(QB):
                    b_round(i * QB + q, i, q, i * QB + q < MB)
            else:
                def step(q, _, i=i):
                    b_round(i * QB + q, i, q, False)
                    return 0

                lax.fori_loop(0, QB, step, 0)

        b_meta(HALF - 1).wait_recv()
        b_meta(HALF).start()

        def tail(t, _):
            for d in range(2):
                b_copy(d, t - MB).wait_recv()
                sb[d, t] = rb[d, t - MB]

                @pl.when(t < TB_R)
                def _():
                    b_copy(d, t).start()

                b_share(d, t).start()
            return 0

        lax.fori_loop(NB_R, SB_R, tail, 0)
        b_meta(HALF).wait_recv()
        for k in range(SECTIONS):
            far = lax.rem(z - lax.rem(owner[k], NZ) + NZ, NZ)
            hops = mb[far]
            meta[0, k : k + 1, :] = hops[SECTIONS + k : SECTIONS + k + 1, :]
            mt[k : k + 1, :] = hops[k : k + 1, :]
        final = remote(mt, meta.at[0], mf_send, mf_recv, sibling)
        final.start()
        for d in range(2):
            all_left(sb.at[d, pl.ds(0, TB_R)], b_send.at[d])
            all_left(sb.at[d, pl.ds(0, SB_R), 0], s_send.at[d])
            all_left(sa.at[d], s_recv.at[d])
        all_left(mb.at[pl.ds(0, NZ - 1)], mr_send)
        all_left(mt, mf_send)
        all_left(mt, mf_recv)

    def a_copy(d, t):
        return remote(sa.at[d, t], ra.at[d, t], a_send.at[d], a_recv.at[d, t], x_to[d])

    def a_share(d, t):
        return remote(sa.at[d, t], sa.at[d, t], s_send.at[d], s_recv.at[d], sibling)

    def a_meta(j):
        return remote(ma.at[j], ma.at[j + 1], mr_send, mr_recv.at[j], x_to[0])

    @pl.when(core == 0)
    def _():
        greet(x_to + [sibling, yl_same, yl_cross, yh_cross])
        hand_over([(xv, sibling, 0), (xa, yl_same, 1), (xv, yh_cross, 2)])

        def at(cc, yy):
            return [owner[k] == (yy * NX + x) * 2 + cc for k in range(SECTIONS)]

        own = [at(0, yl), at(1, yl), at(0, 1 - yl), at(1, 1 - yl)]

        def a_round(t, i, q, first):
            rows = pl.ds(q * CA, CA)
            for d in range(2):
                s0 = i + HALF * d
                if not first:
                    a_copy(d, t - MA).wait_recv()
                had = [(xa[s0, rows, :], xa[s0 + LOW, rows, :])]
                for j in range(3):
                    had.append((pc[j, s0, rows, :], pc[j, s0 + LOW, rows, :]))
                for k in range(SECTIONS):
                    v = had[0][0] if first else ra[d, t - MA, k]
                    for j in range(4):
                        v = pick(high[k], had[j], own[j][k], v)
                    sa[d, t, k] = v
                a_copy(d, t).start()
                a_share(d, t).start()

        for i in range(HALF):
            handed(i)
            if i == 0:
                handed_meta()
                for k in range(SECTIONS):
                    v = mo[0:1, :]
                    for j in range(3):
                        v = jnp.where(own[j + 1][k], mc[j, 0:1, :], v)
                    ma[0, k : k + 1, :] = v
                    ma[0, SECTIONS + k : SECTIONS + k + 1, :] = v
                a_meta(0).start()
            elif i < NX - 1:
                a_meta(i - 1).wait_recv()
                a_meta(i).start()
            if i * QA < MA:
                for q in range(QA):
                    a_round(i * QA + q, i, q, i * QA + q < MA)
            else:
                def step(q, _, i=i):
                    a_round(i * QA + q, i, q, False)
                    return 0

                lax.fori_loop(0, QA, step, 0)

        def tail(t, _):
            for d in range(2):
                a_copy(d, t - MA).wait_recv()
                sa[d, t] = ra[d, t - MA]

                @pl.when(t < TA_R)
                def _():
                    a_copy(d, t).start()

                a_share(d, t).start()
            return 0

        lax.fori_loop(NA_R, SA_R, tail, 0)
        a_meta(NX - 2).wait_recv()
        for k in range(SECTIONS):
            far = lax.rem(x - lax.rem(owner[k] // 2, NX) + NX, NX)
            meta[1, k : k + 1, :] = ma[far][k : k + 1, :]
            mt[k : k + 1, :] = ma[far][k : k + 1, :]
        final = remote(mt, meta.at[1], mf_send, mf_recv, sibling)
        final.start()
        for d in range(2):
            all_left(sa.at[d, pl.ds(0, TA_R)], a_send.at[d])
            all_left(sa.at[d], s_send.at[d])
            all_left(sb.at[d, pl.ds(0, SB_R), 0], s_recv.at[d])
        all_left(ma.at[pl.ds(0, NX - 1)], mr_send)
        all_left(mt, mf_send)
        all_left(mt, mf_recv)

    for j in range(3):
        all_left(pc.at[j], h_send.at[j])
        all_left(mo, mh_send.at[j])


def product_kernel(panels, here, meta, sb, sa, c_ref, a_full, b_full):
    @pl.when(pl.program_id(0) == 0)
    def _():
        row, col = here[0], here[1]
        z, x, core = row % NZ, (col // 2) % NX, col % 2
        a_full[...] = jnp.zeros_like(a_full)
        b_full[...] = jnp.zeros_like(b_full)

        def section(k, _):
            panel = panels[k]
            owner = panel // 2
            high = panel % 2
            zo, xo = owner % NZ, (owner // 2) % NX
            db = [((z - zo + NZ) % NZ) * MB, ((zo - z + NZ) % NZ) * MB]
            da = [((x - xo + NX) % NX) * MA, ((xo - x + NX) % NX) * MA]

            def left(s, n):
                return n + jnp.where((meta[1, k, s] % LC) < PW, 1, 0)

            skip = jnp.where(high == 1, lax.fori_loop(0, SLOTS, left, 0) - LOW, 0)

            def tile(s, w):
                p = meta[0, k, s]

                @pl.when((p // LC) // PW == high)
                def _():
                    wb = s - LOW * high
                    d = wb // HALF
                    t = jnp.where(d == 0, db[0], db[1]) + (wb % HALF) * QB
                    r0 = pl.multiple_of((k * PW + (p // LC) % PW) * BS, BS)
                    c0 = pl.multiple_of((p % LC) * BS, BS)
                    v = sb[d, pl.ds(t, QB), core, k].reshape(BS, BS)
                    b_full[pl.ds(r0, BS), pl.ds(c0, BS)] = v

                p = meta[1, k, s]
                hit = (p % LC) // PW == high

                @pl.when(hit)
                def _():
                    d = w // HALF
                    t = jnp.where(d == 0, da[0], da[1]) + (w % HALF) * QA
                    r0 = pl.multiple_of((p // LC) * BS, BS)
                    c0 = pl.multiple_of((k * PW + (p % LC) % PW) * BS, BS)
                    v = sa[d, pl.ds(t, QA), k].reshape(BS, BS)
                    a_full[pl.ds(r0, BS), pl.ds(c0, BS)] = v

                return w + jnp.where(hit, 1, 0)

            lax.fori_loop(0, SLOTS, tile, skip)
            return 0

        lax.fori_loop(0, SECTIONS, section, 0)

    rows = c_ref.shape[0]
    r0 = pl.multiple_of(pl.program_id(0) * rows, rows)
    c_ref[...] = jnp.dot(
        a_full[pl.ds(r0, rows), :], b_full[...], preferred_element_type=jnp.float32)


def per_device(x_tiles, tile_pos, panel_ids):
    vmem = pl.BlockSpec(memory_space=pltpu.VMEM)
    smem = pl.BlockSpec(memory_space=pltpu.SMEM)
    bf16, i32 = jnp.bfloat16, jnp.int32
    dma = pltpu.SemaphoreType.DMA
    sb, sa, meta = pl.pallas_call(
        comm_kernel,
        out_shape=[
            jax.ShapeDtypeStruct((2, SB_R, 2, SECTIONS, CB, BS), bf16),
            jax.ShapeDtypeStruct((2, SA_R, SECTIONS, CA, BS), bf16),
            jax.ShapeDtypeStruct((2, 8, BS), i32),
        ],
        in_specs=[smem, smem, pl.BlockSpec(memory_space=pl.ANY)],
        out_specs=[vmem, vmem, vmem],
        scratch_shapes=[
            pltpu.VMEM((SLOTS, BS, BS), bf16),
            pltpu.VMEM((SLOTS, BS, BS), bf16),
            pltpu.VMEM((3, SLOTS, BS, BS), bf16),
            pltpu.VMEM((2, TB_R, 2, SECTIONS, CB, BS), bf16),
            pltpu.VMEM((2, TA_R, SECTIONS, CA, BS), bf16),
            pltpu.VMEM((8, BS), i32),
            pltpu.VMEM((3, 8, BS), i32),
            pltpu.VMEM((NZ, 8, BS), i32),
            pltpu.VMEM((NX, 8, BS), i32),
            pltpu.VMEM((8, BS), i32),
            dma, dma((3,)), dma((3, SLOTS)),
            dma((2,)), dma((2, TB_R)), dma((2,)), dma((2, TA_R)), dma((2,)), dma((2,)),
            dma((3,)), dma((3,)), dma, dma((NZ - 1,)), dma, dma,
        ],
        compiler_params=pltpu.CompilerParams(
            collective_id=0, has_side_effects=True, vmem_limit_bytes=40 << 20),
        name="spread_tiles",
    )(panel_ids, tile_pos, x_tiles)
    here = jnp.stack([lax.axis_index("row"), lax.axis_index("col")]).astype(i32)
    n = LR * BS
    kdim = SECTIONS * PW * BS
    steps = 4
    return pl.pallas_call(
        product_kernel,
        out_shape=jax.ShapeDtypeStruct((n, LC * BS), jnp.float32),
        grid=(steps,),
        in_specs=[smem, smem, smem, vmem, vmem],
        out_specs=pl.BlockSpec((n // steps, LC * BS), lambda i: (i, 0)),
        scratch_shapes=[pltpu.VMEM((n, kdim), bf16), pltpu.VMEM((kdim, LC * BS), bf16)],
        compiler_params=pltpu.CompilerParams(vmem_limit_bytes=48 << 20),
        cost_estimate=pl.CostEstimate(
            flops=2 * n * kdim * LC * BS, bytes_accessed=10 << 20, transcendentals=0),
        name="panel_product",
    )(panel_ids, here, meta, sb, sa)


def solution(mesh):
    in_specs = (P("row", "col", None), P("row", "col"), P())
    out_specs = P("row", "col")
    return jax.shard_map(
        per_device, mesh=mesh, in_specs=in_specs, out_specs=out_specs, check_vma=False
    )
```

```python
import jax
import jax.numpy as jnp
from jax import lax
from jax.experimental import pallas as pl
from jax.experimental.pallas import tpu as pltpu
from jax.sharding import PartitionSpec as P

BS = 128
LR = 8
LC = 8
PW = 4
SECTIONS = 4
SLOTS = 16
WIN = 12
HALF = WIN // 2
LOW = SLOTS - WIN
NZ, NX = 8, 4
CB, CA = 16, 32
MB, MA = 7, 5
QB, QA = BS // CB, BS // CA
NB_R, NA_R = HALF * QB, HALF * QA
NRING = 8
TB_R, TA_R = NB_R + (NRING - 2) * MB, NA_R + (NRING - 2) * MA
SB_R, SA_R = TB_R + MB, TA_R + MA
MESH = pl.DeviceIdType.MESH

HANDED = [
    [(s, 0, 64) for s in (0, 4, 6, 10)],
    [(s, 64, 64) for s in (0, 4, 6, 10)],
    [(s, 0, BS) for s in (1, 5, 7, 11)],
    [(s, 0, BS) for s in (2, 8, 12)],
    [(s, 0, BS) for s in (3, 9, 13)],
    [(14, 0, BS)],
    [(15, 0, BS)],
]
PIECES = [piece for group in HANDED for piece in group]


def comm_kernel(
    panels_hbm, pos_hbm, x_hbm, sb, sa, meta,
    panels, pos, xv, xa, pc, rb, ra, mo, mc, mb, mt,
    x_sem, i_sem, h_send, h_recv, b_send, b_recv, a_send, a_recv, s_send, s_recv,
    mh_send, mh_recv, mr_send, mr_recv, mf_send, mf_recv,
):
    row = lax.axis_index("row")
    col = lax.axis_index("col")
    core = lax.rem(col, 2)
    z, yh = lax.rem(row, NZ), row // NZ
    x, yl = lax.rem(col // 2, NX), col // 8
    place = jnp.where(yl == 0, x, NRING - 1 - x)

    def dev(zz, yyh, xx, yyl, cc):
        return {"row": yyh * NZ + zz, "col": (yyl * NX + xx) * 2 + cc}

    def around(step):
        p = lax.rem(place + step, NRING)
        back = p // NX
        return dev(z, yh, jnp.where(back == 0, p, NRING - 1 - p), back, core)

    z_to = [dev(lax.rem(z + 1, NZ), yh, x, yl, core), dev(lax.rem(z + NZ - 1, NZ), yh, x, yl, core)]
    x_to = [around(1), around(NRING - 1)]
    sibling = dev(z, yh, x, yl, 1 - core)
    yh_same, yh_cross = dev(z, 1 - yh, x, yl, core), dev(z, 1 - yh, x, yl, 1 - core)

    def remote(src, dst, send, recv, to):
        return pltpu.make_async_remote_copy(
            src_ref=src, dst_ref=dst, send_sem=send, recv_sem=recv,
            device_id=to, device_id_type=MESH)

    fetch = [
        pltpu.make_async_copy(x_hbm, xv, x_sem),
        pltpu.make_async_copy(panels_hbm, panels, i_sem.at[0]),
        pltpu.make_async_copy(pos_hbm, pos, i_sem.at[1]),
    ]
    for f in fetch:
        f.start()
    barrier = pltpu.get_barrier_semaphore()

    def greet(peers):
        for peer in peers:
            pl.semaphore_signal(barrier, inc=1, device_id=peer, device_id_type=MESH)
        pl.semaphore_wait(barrier, len(peers))
        fetch[0].wait()

    lane = lax.broadcasted_iota(jnp.int32, (8, BS), 1)
    sub = lax.broadcasted_iota(jnp.int32, (8, BS), 0)

    def hand(source, to, j, n):
        s, r, rows = PIECES[n]
        at = (s, pl.ds(r, rows))
        return remote(
            source.at[at], pc.at[(j, *at)], h_send.at[j], h_recv.at[j, n], to)

    def hand_meta(to, j):
        return remote(mo, mc.at[j], mh_send.at[j], mh_recv.at[j], to)

    def hand_over(source, to, j, groups=range(len(HANDED))):
        for g in groups:
            for piece in HANDED[g]:
                hand(source, to, j, PIECES.index(piece)).start()

    def handed(g, js):
        for piece in HANDED[g]:
            for j in js:
                hand(xv, sibling, j, PIECES.index(piece)).wait_recv()

    def all_left(ref, sem):
        pltpu.make_async_copy(ref, ref, sem).wait()

    def pick(own, low_high, cond, v):
        return lax.select(cond, lax.select(own, low_high[1], low_high[0]), v)

    def sort():
        fetch[1].wait()
        fetch[2].wait()
        spot = [pos[0, s] for s in range(SLOTS)]
        right = [lax.rem(p, LC) // PW for p in spot]
        lefts, rights, rank = 0, SLOTS - sum(right), []
        for s in range(SLOTS):
            rank.append(jnp.where(right[s] == 0, lefts, rights))
            lefts, rights = lefts + 1 - right[s], rights + right[s]
        where = jnp.zeros((8, BS), jnp.int32)
        for s in range(SLOTS):
            where = jnp.where((sub == 0) & (lane == s), spot[s], where)
            where = jnp.where((sub == 1) & (lane == rank[s]), spot[s], where)
        mo[...] = where
        for i in range(SLOTS):
            src = sum(jnp.where(rank[s] == i, s, 0) for s in range(SLOTS))
            xa[i] = xv[src]

    def ring_meta(j, to):
        return remote(mb.at[j], mb.at[j + 1], mr_send, mr_recv.at[j], to)

    def finish_meta(part, rows, far, high, unit):
        for k in range(SECTIONS):
            hops = mb[far[k]]
            for cc in range(2):
                line = hops[rows[cc] + k : rows[cc] + k + 1, :]
                lanes = lane[0:1, :]
                line = jnp.where(lanes == SLOTS, jnp.where(high[k], LOW, 0), line)
                line = jnp.where(lanes == SLOTS + 1, far[k] * unit, line)
                line = jnp.where(lanes == SLOTS + 2, lax.rem(NRING - far[k], NRING) * unit, line)
                line = jnp.where(lanes == SLOTS + 3, cc, line)
                line = jnp.where(lanes == SLOTS + 4, jnp.where(high[k], 1, 0), line)
                out = meta.at[part] if part == 1 - cc else mt
                out[k : k + 1, :] = line
        remote(mt, meta.at[part], mf_send, mf_recv, sibling).start()

    def b_copy(d, t):
        return remote(sb.at[d, t], rb.at[d, t], b_send.at[d], b_recv.at[d, t], z_to[d])

    def b_share(d, t):
        return remote(sb.at[d, t, 0], sb.at[d, t, 0], s_send.at[d], s_recv.at[d], sibling)

    @pl.when(core == 1)
    def _():
        greet(z_to + [sibling, yh_same, yh_cross])
        hand_over(xv, yh_same, 1, (0, 1))
        sort()
        owner = [panels[k] // 2 for k in range(SECTIONS)]
        high = [lax.rem(panels[k], 2) == 1 for k in range(SECTIONS)]
        hand_meta(yh_same, 1).start()
        hand_meta(sibling, 0).start()
        hand_over(xa, sibling, 0)
        own_here = [owner[k] == row for k in range(SECTIONS)]
        own_there = [owner[k] == (1 - yh) * NZ + z for k in range(SECTIONS)]

        def b_round(t, i, q, first):
            rows = pl.ds(q * CB, CB)
            for d in range(2):
                s0 = i + HALF * d
                if not first:
                    b_copy(d, t - MB).wait_recv()
                for cc in range(2):
                    if cc == 1:
                        here = [xv[s, rows, :] for s in (s0, s0 + LOW)]
                    else:
                        here = [pc[0, s, rows, :] for s in (s0, s0 + LOW)]
                    there = [pc[2 - cc, s, rows, :] for s in (s0, s0 + LOW)]
                    for k in range(SECTIONS):
                        v = here[0] if first else rb[d, t - MB, cc, k]
                        v = pick(high[k], there, own_there[k], v)
                        v = pick(high[k], here, own_here[k], v)
                        sb[d, t, cc, k] = v
                b_copy(d, t).start()
                b_share(d, t).start()

        for i in range(HALF):
            handed(i + (i > 0), (0, 1, 2))
            hand_over(xv, yh_same, 1, ((2,), (4,), (5, 6))[i] if i < 3 else ())
            if i * QB < MB:
                for q in range(QB):
                    if i == 0 and q == QB // 2:
                        handed(1, (0, 1, 2))
                        hand_over(xv, yh_same, 1, (3,))
                    b_round(i * QB + q, i, q, i * QB + q < MB)
            else:
                def step(q, _, i=i):
                    b_round(i * QB + q, i, q, False)
                    return 0

                lax.fori_loop(0, QB, step, 0)
            if i == 0:
                for j in range(3):
                    hand_meta(sibling, j).wait_recv()
                for cc in range(2):
                    here = mo[0:1, :] if cc == 1 else mc[0, 0:1, :]
                    there = mc[2 - cc, 0:1, :]
                    for k in range(SECTIONS):
                        r = cc * SECTIONS + k
                        mb[0, r : r + 1, :] = jnp.where(own_here[k], here, there)
            else:
                ring_meta(i - 1, z_to[0]).wait_recv()
            ring_meta(i, z_to[0]).start()

        def tail(t, _):
            for d in range(2):
                b_copy(d, t - MB).wait_recv()
                sb[d, t] = rb[d, t - MB]

                @pl.when(t < TB_R)
                def _():
                    b_copy(d, t).start()

                b_share(d, t).start()
            return 0

        lax.fori_loop(NB_R, NB_R + MB, tail, 0)
        ring_meta(HALF - 1, z_to[0]).wait_recv()
        ring_meta(HALF, z_to[0]).start()
        lax.fori_loop(NB_R + MB, NB_R + 5 * MB, tail, 0)
        ring_meta(HALF, z_to[0]).wait_recv()
        far = [lax.rem(z - lax.rem(owner[k], NZ) + NZ, NZ) for k in range(SECTIONS)]
        finish_meta(0, (0, SECTIONS), far, high, MB)
        lax.fori_loop(NB_R + 5 * MB, SB_R, tail, 0)
        for d in range(2):
            all_left(sb.at[d, pl.ds(0, TB_R)], b_send.at[d])
            all_left(sb.at[d, pl.ds(0, SB_R), 0], s_send.at[d])
            all_left(sa.at[d], s_recv.at[d])
        for j in (0, 1):
            all_left(pc.at[j], h_send.at[j])
            all_left(mo, mh_send.at[j])

    def a_copy(d, t):
        return remote(sa.at[d, t], ra.at[d, t], a_send.at[d], a_recv.at[d, t], x_to[d])

    def a_share(d, t):
        return remote(sa.at[d, t], sa.at[d, t], s_send.at[d], s_recv.at[d], sibling)

    @pl.when(core == 0)
    def _():
        greet(x_to + [sibling, yh_cross])
        hand_over(xv, yh_cross, 2, (0, 1))
        hand_over(xv, sibling, 0)
        sort()
        owner = [panels[k] // 2 for k in range(SECTIONS)]
        high = [lax.rem(panels[k], 2) == 1 for k in range(SECTIONS)]
        hand_meta(yh_cross, 2).start()
        hand_meta(sibling, 0).start()
        own_here = [owner[k] == col for k in range(SECTIONS)]
        own_there = [owner[k] == col + 1 for k in range(SECTIONS)]

        def a_round(t, i, q, first):
            rows = pl.ds(q * CA, CA)
            for d in range(2):
                s0 = i + HALF * d
                if not first:
                    a_copy(d, t - MA).wait_recv()
                here = [xa[s, rows, :] for s in (s0, s0 + LOW)]
                there = [pc[0, s, rows, :] for s in (s0, s0 + LOW)]
                for k in range(SECTIONS):
                    v = here[0] if first else ra[d, t - MA, k]
                    v = pick(high[k], there, own_there[k], v)
                    v = pick(high[k], here, own_here[k], v)
                    sa[d, t, k] = v
                a_copy(d, t).start()
                a_share(d, t).start()

        for i in range(HALF):
            handed(i + (i > 0), (0,))
            hand_over(xv, yh_cross, 2, ((2,), (4,), (5, 6))[i] if i < 3 else ())
            if i * QA < MA:
                for q in range(QA):
                    if i == 0 and q == QA // 2:
                        handed(1, (0,))
                        hand_over(xv, yh_cross, 2, (3,))
                    a_round(i * QA + q, i, q, i * QA + q < MA)
            else:
                def step(q, _, i=i):
                    a_round(i * QA + q, i, q, False)
                    return 0

                lax.fori_loop(0, QA, step, 0)
            if i == 0:
                hand_meta(sibling, 0).wait_recv()
                for k in range(SECTIONS):
                    mb[0, k : k + 1, :] = jnp.where(own_here[k], mo[1:2, :], mc[0, 1:2, :])
                    mb[0, SECTIONS + k : SECTIONS + k + 1, :] = mo[0:1, :]
            else:
                ring_meta(i - 1, x_to[0]).wait_recv()
            ring_meta(i, x_to[0]).start()

        def tail(t, _):
            for d in range(2):
                a_copy(d, t - MA).wait_recv()
                sa[d, t] = ra[d, t - MA]

                @pl.when(t < TA_R)
                def _():
                    a_copy(d, t).start()

                a_share(d, t).start()
            return 0

        lax.fori_loop(NA_R, NA_R + MA, tail, 0)
        ring_meta(HALF - 1, x_to[0]).wait_recv()
        ring_meta(HALF, x_to[0]).start()
        lax.fori_loop(NA_R + MA, NA_R + 5 * MA, tail, 0)
        ring_meta(HALF, x_to[0]).wait_recv()
        far = []
        for k in range(SECTIONS):
            xo, yo = lax.rem(owner[k] // 2, NX), owner[k] // 8
            far.append(lax.rem(place - jnp.where(yo == 0, xo, NRING - 1 - xo) + NRING, NRING))
        finish_meta(1, (0, 0), far, high, MA)
        lax.fori_loop(NA_R + 5 * MA, SA_R, tail, 0)
        for d in range(2):
            all_left(sa.at[d, pl.ds(0, TA_R)], a_send.at[d])
            all_left(sa.at[d], s_send.at[d])
            all_left(sb.at[d, pl.ds(0, SB_R), 0], s_recv.at[d])
        for j in (0, 2):
            all_left(pc.at[j], h_send.at[j])
            all_left(mo, mh_send.at[j])

    all_left(mb.at[pl.ds(0, NRING - 1)], mr_send)
    all_left(mt, mf_send)
    all_left(mt, mf_recv)


def product_kernel(meta, sb, sa, c_ref, a_full, b_full):
    @pl.when(pl.program_id(0) == 0)
    def _():
        a_full[...] = jnp.zeros_like(a_full)
        b_full[...] = jnp.zeros_like(b_full)

        def section(k, _):
            for part in range(2):
                low = meta[part, k, SLOTS]
                start = [meta[part, k, SLOTS + 1], meta[part, k, SLOTS + 2]]
                core = meta[part, k, SLOTS + 3]
                high = meta[part, k, SLOTS + 4]
                for w in range(WIN):
                    p = meta[part, k, low + w]
                    d = w // HALF
                    if part == 0:
                        @pl.when((p >> 5) == high)
                        def _(p=p, d=d, w=w, start=start, core=core):
                            v = sb[d, pl.ds(start[d] + (w % HALF) * QB, QB), core, k]
                            r0 = pl.multiple_of((k * PW + ((p >> 3) & 3)) * BS, BS)
                            c0 = pl.multiple_of((p & 7) * BS, BS)
                            b_full[pl.ds(r0, BS), pl.ds(c0, BS)] = v.reshape(BS, BS)
                    else:
                        @pl.when(((p >> 2) & 1) == high)
                        def _(p=p, d=d, w=w, start=start):
                            v = sa[d, pl.ds(start[d] + (w % HALF) * QA, QA), k]
                            r0 = pl.multiple_of((p >> 3) * BS, BS)
                            c0 = pl.multiple_of((k * PW + (p & 3)) * BS, BS)
                            a_full[pl.ds(r0, BS), pl.ds(c0, BS)] = v.reshape(BS, BS)
            return 0

        lax.fori_loop(0, SECTIONS, section, 0)

    rows = c_ref.shape[0]
    r0 = pl.multiple_of(pl.program_id(0) * rows, rows)
    c_ref[...] = jnp.dot(
        a_full[pl.ds(r0, rows), :], b_full[...], preferred_element_type=jnp.float32)


def per_device(x_tiles, tile_pos, panel_ids):
    vmem = pl.BlockSpec(memory_space=pltpu.VMEM)
    smem = pl.BlockSpec(memory_space=pltpu.SMEM)
    hbm = pl.BlockSpec(memory_space=pltpu.HBM)
    bf16, i32 = jnp.bfloat16, jnp.int32
    dma = pltpu.SemaphoreType.DMA
    sb, sa, meta = pl.pallas_call(
        comm_kernel,
        out_shape=[
            jax.ShapeDtypeStruct((2, SB_R, 2, SECTIONS, CB, BS), bf16),
            jax.ShapeDtypeStruct((2, SA_R, SECTIONS, CA, BS), bf16),
            jax.ShapeDtypeStruct((2, 8, BS), i32),
        ],
        in_specs=[hbm, hbm, hbm],
        out_specs=[vmem, vmem, vmem],
        scratch_shapes=[
            pltpu.SMEM((SECTIONS,), i32),
            pltpu.SMEM((1, SLOTS), i32),
            pltpu.VMEM((SLOTS, BS, BS), bf16),
            pltpu.VMEM((SLOTS, BS, BS), bf16),
            pltpu.VMEM((3, SLOTS, BS, BS), bf16),
            pltpu.VMEM((2, TB_R, 2, SECTIONS, CB, BS), bf16),
            pltpu.VMEM((2, TA_R, SECTIONS, CA, BS), bf16),
            pltpu.VMEM((8, BS), i32),
            pltpu.VMEM((3, 8, BS), i32),
            pltpu.VMEM((NRING, 8, BS), i32),
            pltpu.VMEM((8, BS), i32),
            dma, dma((2,)), dma((3,)), dma((3, len(PIECES))),
            dma((2,)), dma((2, TB_R)), dma((2,)), dma((2, TA_R)), dma((2,)), dma((2,)),
            dma((3,)), dma((3,)), dma, dma((NRING - 1,)), dma, dma,
        ],
        compiler_params=pltpu.CompilerParams(
            collective_id=0, has_side_effects=True, vmem_limit_bytes=28 << 20),
        name="spread_tiles",
    )(*[
        pltpu.with_memory_space_constraint(v, pltpu.HBM)
        for v in (panel_ids, tile_pos, x_tiles)
    ])
    n = LR * BS
    kdim = SECTIONS * PW * BS
    steps = 4
    return pl.pallas_call(
        product_kernel,
        out_shape=jax.ShapeDtypeStruct((n, LC * BS), jnp.float32),
        grid=(steps,),
        in_specs=[smem, vmem, vmem],
        out_specs=pl.BlockSpec((n // steps, LC * BS), lambda i: (i, 0)),
        scratch_shapes=[pltpu.VMEM((n, kdim), bf16), pltpu.VMEM((kdim, LC * BS), bf16)],
        compiler_params=pltpu.CompilerParams(vmem_limit_bytes=16 << 20),
        cost_estimate=pl.CostEstimate(
            flops=2 * n * kdim * LC * BS, bytes_accessed=10 << 20, transcendentals=0),
        name="panel_product",
    )(meta, sb, sa)


def solution(mesh):
    in_specs = (P("row", "col", None), P("row", "col"), P())
    out_specs = P("row", "col")
    return jax.shard_map(
        per_device, mesh=mesh, in_specs=in_specs, out_specs=out_specs, check_vma=False
    )
```

```python
import jax
import jax.numpy as jnp
from jax import lax
from jax.experimental import pallas as pl
from jax.experimental.pallas import tpu as pltpu
from jax.sharding import PartitionSpec as P

BS = 128
LR = 8
LC = 8
PW = 4
SECTIONS = 4
SLOTS = 16
WIN = 12
HALF = WIN // 2
LOW = SLOTS - WIN
NZ, NX = 8, 4
CB, CA = 16, 32
MB, MA = 7, 5
QB, QA = BS // CB, BS // CA
NB_R, NA_R = HALF * QB, HALF * QA
NRING = 8
TB_R, TA_R = NB_R + (NRING - 2) * MB, NA_R + (NRING - 2) * MA
SB_R, SA_R = TB_R + MB, TA_R + MA
MESH = pl.DeviceIdType.MESH

def slots_of(i, d):
    if i < (WIN - LOW) // 2:
        return [LOW + 2 * i + d]
    s = 2 * (i - (WIN - LOW) // 2) + d
    return [s, WIN + s]


FIRST = 32
HANDED = [
    [(s, 0, FIRST) for d in range(2) for s in slots_of(0, d)],
    [(s, FIRST, BS - FIRST) for d in range(2) for s in slots_of(0, d)],
]
for _i in range(1, HALF):
    HANDED.append([(s, 0, BS) for d in range(2) for s in slots_of(_i, d)])
PIECES = [piece for group in HANDED for piece in group]


def comm_kernel(
    panels_hbm, pos_hbm, x_hbm, sb, sa, meta,
    panels, pos, xv, xa, pc, rb, ra, mo, mc, mb, mt,
    x_sem, i_sem, h_send, h_recv, b_send, b_recv, a_send, a_recv, s_send, s_recv,
    mh_send, mh_recv, mr_send, mr_recv, mf_send, mf_recv,
):
    row = lax.axis_index("row")
    col = lax.axis_index("col")
    core = lax.rem(col, 2)
    z, yh = lax.rem(row, NZ), row // NZ
    x, yl = lax.rem(col // 2, NX), col // 8
    place = jnp.where(yl == 0, x, NRING - 1 - x)

    def dev(zz, yyh, xx, yyl, cc):
        return {"row": yyh * NZ + zz, "col": (yyl * NX + xx) * 2 + cc}

    def around(step):
        p = lax.rem(place + step, NRING)
        back = p // NX
        return dev(z, yh, jnp.where(back == 0, p, NRING - 1 - p), back, core)

    z_to = [dev(lax.rem(z + 1, NZ), yh, x, yl, core), dev(lax.rem(z + NZ - 1, NZ), yh, x, yl, core)]
    x_to = [around(1), around(NRING - 1)]
    sibling = dev(z, yh, x, yl, 1 - core)
    yh_same, yh_cross = dev(z, 1 - yh, x, yl, core), dev(z, 1 - yh, x, yl, 1 - core)

    def remote(src, dst, send, recv, to):
        return pltpu.make_async_remote_copy(
            src_ref=src, dst_ref=dst, send_sem=send, recv_sem=recv,
            device_id=to, device_id_type=MESH)

    fetch = [
        pltpu.make_async_copy(x_hbm, xv, x_sem),
        pltpu.make_async_copy(panels_hbm, panels, i_sem.at[0]),
        pltpu.make_async_copy(pos_hbm, pos, i_sem.at[1]),
    ]
    for f in fetch:
        f.start()
    barrier = pltpu.get_barrier_semaphore()

    def greet(peers):
        for peer in peers:
            pl.semaphore_signal(barrier, inc=1, device_id=peer, device_id_type=MESH)
        pl.semaphore_wait(barrier, len(peers))
        fetch[0].wait()

    lane = lax.broadcasted_iota(jnp.int32, (8, BS), 1)
    sub = lax.broadcasted_iota(jnp.int32, (8, BS), 0)

    def hand(source, to, j, n):
        s, r, rows = PIECES[n]
        at = (s, pl.ds(r, rows))
        return remote(
            source.at[at], pc.at[(j, *at)], h_send.at[j], h_recv.at[j, n], to)

    def hand_meta(to, j):
        return remote(mo, mc.at[j], mh_send.at[j], mh_recv.at[j], to)

    def hand_over(source, to, j, groups=range(len(HANDED))):
        for g in groups:
            for piece in HANDED[g]:
                hand(source, to, j, PIECES.index(piece)).start()

    def handed(g, js):
        for piece in HANDED[g]:
            for j in js:
                hand(xv, sibling, j, PIECES.index(piece)).wait_recv()

    def all_left(ref, sem):
        pltpu.make_async_copy(ref, ref, sem).wait()

    def pick(own, low_high, cond, v):
        mine = low_high[0]
        if len(low_high) == 2:
            mine = lax.select(own, low_high[1], mine)
        return lax.select(cond, mine, v)

    def sort():
        fetch[1].wait()
        fetch[2].wait()
        spot = [pos[0, s] for s in range(SLOTS)]
        right = [lax.rem(p, LC) // PW for p in spot]
        lefts, rights, rank = 0, SLOTS - sum(right), []
        for s in range(SLOTS):
            rank.append(jnp.where(right[s] == 0, lefts, rights))
            lefts, rights = lefts + 1 - right[s], rights + right[s]
        where = jnp.zeros((8, BS), jnp.int32)
        for s in range(SLOTS):
            where = jnp.where((sub == 0) & (lane == s), spot[s], where)
            where = jnp.where((sub == 1) & (lane == rank[s]), spot[s], where)
        mo[...] = where
        for i in range(SLOTS):
            src = sum(jnp.where(rank[s] == i, s, 0) for s in range(SLOTS))
            xa[i] = xv[src]

    def ring_meta(j, to):
        return remote(mb.at[j], mb.at[j + 1], mr_send, mr_recv.at[j], to)

    def finish_meta(part, rows, far, high, unit):
        for k in range(SECTIONS):
            hops = mb[far[k]]
            for cc in range(2):
                line = hops[rows[cc] + k : rows[cc] + k + 1, :]
                lanes = lane[0:1, :]
                line = jnp.where(lanes == SLOTS, jnp.where(high[k], WIN, 0), line)
                line = jnp.where(lanes == SLOTS + 1, far[k] * unit, line)
                line = jnp.where(lanes == SLOTS + 2, lax.rem(NRING - far[k], NRING) * unit, line)
                line = jnp.where(lanes == SLOTS + 3, cc, line)
                line = jnp.where(lanes == SLOTS + 4, jnp.where(high[k], 1, 0), line)
                out = meta.at[part] if part == 1 - cc else mt
                out[k : k + 1, :] = line
        remote(mt, meta.at[part], mf_send, mf_recv, sibling).start()

    def b_copy(d, t):
        return remote(sb.at[d, t], rb.at[d, t], b_send.at[d], b_recv.at[d, t], z_to[d])

    def b_share(d, t):
        return remote(sb.at[d, t, 0], sb.at[d, t, 0], s_send.at[d], s_recv.at[d], sibling)

    @pl.when(core == 1)
    def _():
        greet(z_to + [sibling, yh_same, yh_cross])
        hand_over(xv, yh_same, 1, (0, 1, 2))
        sort()
        owner = [panels[k] // 2 for k in range(SECTIONS)]
        high = [lax.rem(panels[k], 2) == 1 for k in range(SECTIONS)]
        hand_meta(yh_same, 1).start()
        hand_meta(sibling, 0).start()
        hand_over(xa, sibling, 0)
        own_here = [owner[k] == row for k in range(SECTIONS)]
        own_there = [owner[k] == (1 - yh) * NZ + z for k in range(SECTIONS)]

        def b_round(t, i, q, first):
            rows = pl.ds(q * CB, CB)
            for d in range(2):
                slots = slots_of(i, d)
                if not first:
                    b_copy(d, t - MB).wait_recv()
                for cc in range(2):
                    if cc == 1:
                        here = [xv[s, rows, :] for s in slots]
                    else:
                        here = [pc[0, s, rows, :] for s in slots]
                    there = [pc[2 - cc, s, rows, :] for s in slots]
                    for k in range(SECTIONS):
                        v = here[0] if first else rb[d, t - MB, cc, k]
                        v = pick(high[k], there, own_there[k], v)
                        v = pick(high[k], here, own_here[k], v)
                        sb[d, t, cc, k] = v
                b_copy(d, t).start()
                b_share(d, t).start()

        for i in range(HALF):
            handed(i + (i > 0), (0, 1, 2))
            hand_over(xv, yh_same, 1, ((3,), (5,), (6,))[i] if i < 3 else ())
            if i * QB < MB:
                for q in range(QB):
                    if i == 0 and q == FIRST // CB:
                        handed(1, (0, 1, 2))
                        hand_over(xv, yh_same, 1, (4,))
                    b_round(i * QB + q, i, q, i * QB + q < MB)
            else:
                def step(q, _, i=i):
                    b_round(i * QB + q, i, q, False)
                    return 0

                lax.fori_loop(0, QB, step, 0)
            if i == 0:
                for j in range(3):
                    hand_meta(sibling, j).wait_recv()
                for cc in range(2):
                    here = mo[0:1, :] if cc == 1 else mc[0, 0:1, :]
                    there = mc[2 - cc, 0:1, :]
                    for k in range(SECTIONS):
                        r = cc * SECTIONS + k
                        mb[0, r : r + 1, :] = jnp.where(own_here[k], here, there)
            else:
                ring_meta(i - 1, z_to[0]).wait_recv()
            ring_meta(i, z_to[0]).start()

        def tail(t, _):
            for d in range(2):
                b_copy(d, t - MB).wait_recv()
                sb[d, t] = rb[d, t - MB]

                @pl.when(t < TB_R)
                def _():
                    b_copy(d, t).start()

                b_share(d, t).start()
            return 0

        lax.fori_loop(NB_R, NB_R + MB, tail, 0)
        ring_meta(HALF - 1, z_to[0]).wait_recv()
        ring_meta(HALF, z_to[0]).start()
        lax.fori_loop(NB_R + MB, NB_R + 5 * MB, tail, 0)
        ring_meta(HALF, z_to[0]).wait_recv()
        far = [lax.rem(z - lax.rem(owner[k], NZ) + NZ, NZ) for k in range(SECTIONS)]
        finish_meta(0, (0, SECTIONS), far, high, MB)
        lax.fori_loop(NB_R + 5 * MB, SB_R, tail, 0)
        for d in range(2):
            all_left(sb.at[d, pl.ds(0, TB_R)], b_send.at[d])
            all_left(sb.at[d, pl.ds(0, SB_R), 0], s_send.at[d])
            all_left(sa.at[d], s_recv.at[d])
        for j in (0, 1):
            all_left(pc.at[j], h_send.at[j])
            all_left(mo, mh_send.at[j])

    def a_copy(d, t):
        return remote(sa.at[d, t], ra.at[d, t], a_send.at[d], a_recv.at[d, t], x_to[d])

    def a_share(d, t):
        return remote(sa.at[d, t], sa.at[d, t], s_send.at[d], s_recv.at[d], sibling)

    @pl.when(core == 0)
    def _():
        greet(x_to + [sibling, yh_cross])
        hand_over(xv, yh_cross, 2, (0, 1, 2))
        hand_over(xv, sibling, 0)
        sort()
        owner = [panels[k] // 2 for k in range(SECTIONS)]
        high = [lax.rem(panels[k], 2) == 1 for k in range(SECTIONS)]
        hand_meta(yh_cross, 2).start()
        hand_meta(sibling, 0).start()
        own_here = [owner[k] == col for k in range(SECTIONS)]
        own_there = [owner[k] == col + 1 for k in range(SECTIONS)]

        def a_round(t, i, q, first):
            rows = pl.ds(q * CA, CA)
            for d in range(2):
                slots = slots_of(i, d)
                if not first:
                    a_copy(d, t - MA).wait_recv()
                here = [xa[s, rows, :] for s in slots]
                there = [pc[0, s, rows, :] for s in slots]
                for k in range(SECTIONS):
                    v = here[0] if first else ra[d, t - MA, k]
                    v = pick(high[k], there, own_there[k], v)
                    v = pick(high[k], here, own_here[k], v)
                    sa[d, t, k] = v
                a_copy(d, t).start()
                a_share(d, t).start()

        for i in range(HALF):
            handed(i + (i > 0), (0,))
            hand_over(xv, yh_cross, 2, ((3,), (5,), (6,))[i] if i < 3 else ())
            if i * QA < MA:
                for q in range(QA):
                    if i == 0 and q == FIRST // CA:
                        handed(1, (0,))
                        hand_over(xv, yh_cross, 2, (4,))
                    a_round(i * QA + q, i, q, i * QA + q < MA)
            else:
                def step(q, _, i=i):
                    a_round(i * QA + q, i, q, False)
                    return 0

                lax.fori_loop(0, QA, step, 0)
            if i == 0:
                hand_meta(sibling, 0).wait_recv()
                for k in range(SECTIONS):
                    mb[0, k : k + 1, :] = jnp.where(own_here[k], mo[1:2, :], mc[0, 1:2, :])
                    mb[0, SECTIONS + k : SECTIONS + k + 1, :] = mo[0:1, :]
            else:
                ring_meta(i - 1, x_to[0]).wait_recv()
            ring_meta(i, x_to[0]).start()

        def tail(t, _):
            for d in range(2):
                a_copy(d, t - MA).wait_recv()
                sa[d, t] = ra[d, t - MA]

                @pl.when(t < TA_R)
                def _():
                    a_copy(d, t).start()

                a_share(d, t).start()
            return 0

        lax.fori_loop(NA_R, NA_R + MA, tail, 0)
        ring_meta(HALF - 1, x_to[0]).wait_recv()
        ring_meta(HALF, x_to[0]).start()
        lax.fori_loop(NA_R + MA, NA_R + 5 * MA, tail, 0)
        ring_meta(HALF, x_to[0]).wait_recv()
        far = []
        for k in range(SECTIONS):
            xo, yo = lax.rem(owner[k] // 2, NX), owner[k] // 8
            far.append(lax.rem(place - jnp.where(yo == 0, xo, NRING - 1 - xo) + NRING, NRING))
        finish_meta(1, (0, 0), far, high, MA)
        lax.fori_loop(NA_R + 5 * MA, SA_R, tail, 0)
        for d in range(2):
            all_left(sa.at[d, pl.ds(0, TA_R)], a_send.at[d])
            all_left(sa.at[d], s_send.at[d])
            all_left(sb.at[d, pl.ds(0, SB_R), 0], s_recv.at[d])
        for j in (0, 2):
            all_left(pc.at[j], h_send.at[j])
            all_left(mo, mh_send.at[j])

    all_left(mb.at[pl.ds(0, NRING - 1)], mr_send)
    all_left(mt, mf_send)
    all_left(mt, mf_recv)


def product_kernel(meta, sb, sa, c_ref, a_full, b_full):
    @pl.when(pl.program_id(0) == 0)
    def _():
        a_full[...] = jnp.zeros_like(a_full)
        b_full[...] = jnp.zeros_like(b_full)

        def section(k, _):
            for part in range(2):
                late = meta[part, k, SLOTS]
                start = [meta[part, k, SLOTS + 1], meta[part, k, SLOTS + 2]]
                core = meta[part, k, SLOTS + 3]
                high = meta[part, k, SLOTS + 4]
                for w in range(WIN):
                    d = w // HALF
                    slots = slots_of(w % HALF, d)
                    p = meta[part, k, slots[0] + (late if len(slots) == 2 else 0)]
                    if part == 0:
                        @pl.when((p >> 5) == high)
                        def _(p=p, d=d, w=w, start=start, core=core):
                            v = sb[d, pl.ds(start[d] + (w % HALF) * QB, QB), core, k]
                            r0 = pl.multiple_of((k * PW + ((p >> 3) & 3)) * BS, BS)
                            c0 = pl.multiple_of((p & 7) * BS, BS)
                            b_full[pl.ds(r0, BS), pl.ds(c0, BS)] = v.reshape(BS, BS)
                    else:
                        @pl.when(((p >> 2) & 1) == high)
                        def _(p=p, d=d, w=w, start=start):
                            v = sa[d, pl.ds(start[d] + (w % HALF) * QA, QA), k]
                            r0 = pl.multiple_of((p >> 3) * BS, BS)
                            c0 = pl.multiple_of((k * PW + (p & 3)) * BS, BS)
                            a_full[pl.ds(r0, BS), pl.ds(c0, BS)] = v.reshape(BS, BS)
            return 0

        lax.fori_loop(0, SECTIONS, section, 0)

    rows = c_ref.shape[0]
    r0 = pl.multiple_of(pl.program_id(0) * rows, rows)
    c_ref[...] = jnp.dot(
        a_full[pl.ds(r0, rows), :], b_full[...], preferred_element_type=jnp.float32)


def per_device(x_tiles, tile_pos, panel_ids):
    vmem = pl.BlockSpec(memory_space=pltpu.VMEM)
    smem = pl.BlockSpec(memory_space=pltpu.SMEM)
    hbm = pl.BlockSpec(memory_space=pltpu.HBM)
    bf16, i32 = jnp.bfloat16, jnp.int32
    dma = pltpu.SemaphoreType.DMA
    sb, sa, meta = pl.pallas_call(
        comm_kernel,
        out_shape=[
            jax.ShapeDtypeStruct((2, SB_R, 2, SECTIONS, CB, BS), bf16),
            jax.ShapeDtypeStruct((2, SA_R, SECTIONS, CA, BS), bf16),
            jax.ShapeDtypeStruct((2, 8, BS), i32),
        ],
        in_specs=[hbm, hbm, hbm],
        out_specs=[vmem, vmem, vmem],
        scratch_shapes=[
            pltpu.SMEM((SECTIONS,), i32),
            pltpu.SMEM((1, SLOTS), i32),
            pltpu.VMEM((SLOTS, BS, BS), bf16),
            pltpu.VMEM((SLOTS, BS, BS), bf16),
            pltpu.VMEM((3, SLOTS, BS, BS), bf16),
            pltpu.VMEM((2, TB_R, 2, SECTIONS, CB, BS), bf16),
            pltpu.VMEM((2, TA_R, SECTIONS, CA, BS), bf16),
            pltpu.VMEM((8, BS), i32),
            pltpu.VMEM((3, 8, BS), i32),
            pltpu.VMEM((NRING, 8, BS), i32),
            pltpu.VMEM((8, BS), i32),
            dma, dma((2,)), dma((3,)), dma((3, len(PIECES))),
            dma((2,)), dma((2, TB_R)), dma((2,)), dma((2, TA_R)), dma((2,)), dma((2,)),
            dma((3,)), dma((3,)), dma, dma((NRING - 1,)), dma, dma,
        ],
        compiler_params=pltpu.CompilerParams(
            collective_id=0, has_side_effects=True, vmem_limit_bytes=28 << 20),
        name="spread_tiles",
    )(*[
        pltpu.with_memory_space_constraint(v, pltpu.HBM)
        for v in (panel_ids, tile_pos, x_tiles)
    ])
    n = LR * BS
    kdim = SECTIONS * PW * BS
    steps = 4
    return pl.pallas_call(
        product_kernel,
        out_shape=jax.ShapeDtypeStruct((n, LC * BS), jnp.float32),
        grid=(steps,),
        in_specs=[smem, vmem, vmem],
        out_specs=pl.BlockSpec((n // steps, LC * BS), lambda i: (i, 0)),
        scratch_shapes=[pltpu.VMEM((n, kdim), bf16), pltpu.VMEM((kdim, LC * BS), bf16)],
        compiler_params=pltpu.CompilerParams(vmem_limit_bytes=16 << 20),
        cost_estimate=pl.CostEstimate(
            flops=2 * n * kdim * LC * BS, bytes_accessed=10 << 20, transcendentals=0),
        name="panel_product",
    )(meta, sb, sa)


def solution(mesh):
    in_specs = (P("row", "col", None), P("row", "col"), P())
    out_specs = P("row", "col")
    return jax.shard_map(
        per_device, mesh=mesh, in_specs=in_specs, out_specs=out_specs, check_vma=False
    )
```

```python
import jax
import jax.numpy as jnp
from jax import lax
from jax.experimental import pallas as pl
from jax.experimental.pallas import tpu as pltpu
from jax.sharding import PartitionSpec as P

BS = 128
LR = 8
LC = 8
PW = 4
SECTIONS = 4
SLOTS = 16
WIN = 12
HALF = WIN // 2
LOW = SLOTS - WIN
NZ, NX = 8, 4
CB, CA = 16, 32
MB, MA = 7, 5
QB, QA = BS // CB, BS // CA
NB_R, NA_R = HALF * QB, HALF * QA
NRING = 8
TB_R, TA_R = NB_R + (NRING - 2) * MB, NA_R + (NRING - 2) * MA
SB_R, SA_R = TB_R + MB, TA_R + MA
MESH = pl.DeviceIdType.MESH

def slots_of(i, d):
    if i < (WIN - LOW) // 2:
        return [LOW + 2 * i + d]
    s = 2 * (i - (WIN - LOW) // 2) + d
    return [s, WIN + s]


FIRST = 32
HANDED = [
    [(s, 0, FIRST) for d in range(2) for s in slots_of(0, d)],
    [(s, FIRST, BS - FIRST) for d in range(2) for s in slots_of(0, d)],
]
for _i in range(1, HALF):
    HANDED.append([(s, 0, BS) for d in range(2) for s in slots_of(_i, d)])
PIECES = [piece for group in HANDED for piece in group]


def comm_kernel(
    panels_hbm, pos_hbm, x_hbm, sb, sa, meta,
    panels, pos, xv, xa, pc, rb, ra, mo, mc, mb, mt,
    x_sem, i_sem, h_send, h_recv, b_send, b_recv, a_send, a_recv, s_send, s_recv,
    mh_send, mh_recv, mr_send, mr_recv, mf_send, mf_recv,
):
    row = lax.axis_index("row")
    col = lax.axis_index("col")
    core = lax.rem(col, 2)
    z, yh = lax.rem(row, NZ), row // NZ
    x, yl = lax.rem(col // 2, NX), col // 8
    place = jnp.where(yl == 0, x, NRING - 1 - x)

    def dev(zz, yyh, xx, yyl, cc):
        return {"row": yyh * NZ + zz, "col": (yyl * NX + xx) * 2 + cc}

    def around(step):
        p = lax.rem(place + step, NRING)
        back = p // NX
        return dev(z, yh, jnp.where(back == 0, p, NRING - 1 - p), back, core)

    z_to = [dev(lax.rem(z + 1, NZ), yh, x, yl, core), dev(lax.rem(z + NZ - 1, NZ), yh, x, yl, core)]
    x_to = [around(1), around(NRING - 1)]
    sibling = dev(z, yh, x, yl, 1 - core)
    yh_same, yh_cross = dev(z, 1 - yh, x, yl, core), dev(z, 1 - yh, x, yl, 1 - core)

    def remote(src, dst, send, recv, to):
        return pltpu.make_async_remote_copy(
            src_ref=src, dst_ref=dst, send_sem=send, recv_sem=recv,
            device_id=to, device_id_type=MESH)

    fetch = [
        pltpu.make_async_copy(x_hbm, xv, x_sem),
        pltpu.make_async_copy(panels_hbm, panels, i_sem.at[0]),
        pltpu.make_async_copy(pos_hbm, pos, i_sem.at[1]),
    ]
    for f in fetch:
        f.start()
    barrier = pltpu.get_barrier_semaphore()

    def greet(peers):
        for peer in peers:
            pl.semaphore_signal(barrier, inc=1, device_id=peer, device_id_type=MESH)
        pl.semaphore_wait(barrier, len(peers))
        fetch[0].wait()

    lane = lax.broadcasted_iota(jnp.int32, (8, BS), 1)
    sub = lax.broadcasted_iota(jnp.int32, (8, BS), 0)

    def hand(source, to, j, n):
        s, r, rows = PIECES[n]
        at = (s, pl.ds(r, rows))
        return remote(
            source.at[at], pc.at[(j, *at)], h_send.at[j], h_recv.at[j, n], to)

    def hand_meta(to, j):
        return remote(mo, mc.at[j], mh_send.at[j], mh_recv.at[j], to)

    def hand_over(source, to, j, groups=range(len(HANDED))):
        for g in groups:
            for piece in HANDED[g]:
                hand(source, to, j, PIECES.index(piece)).start()

    def handed(g, js):
        for piece in HANDED[g]:
            for j in js:
                hand(xv, sibling, j, PIECES.index(piece)).wait_recv()

    def all_left(ref, sem):
        pltpu.make_async_copy(ref, ref, sem).wait()

    def pick(own, low_high, cond, v):
        mine = low_high[0]
        if len(low_high) == 2:
            mine = lax.select(own, low_high[1], mine)
        return lax.select(cond, mine, v)

    def sort():
        fetch[1].wait()
        fetch[2].wait()
        spot = [pos[0, s] for s in range(SLOTS)]
        right = [lax.rem(p, LC) // PW for p in spot]
        lefts, rights, rank = 0, SLOTS - sum(right), []
        for s in range(SLOTS):
            rank.append(jnp.where(right[s] == 0, lefts, rights))
            lefts, rights = lefts + 1 - right[s], rights + right[s]
        where = jnp.zeros((8, BS), jnp.int32)
        for s in range(SLOTS):
            where = jnp.where((sub == 0) & (lane == s), spot[s], where)
            where = jnp.where((sub == 1) & (lane == rank[s]), spot[s], where)
        mo[...] = where
        for i in range(SLOTS):
            src = sum(jnp.where(rank[s] == i, s, 0) for s in range(SLOTS))
            xa[i] = xv[src]

    def ring_meta(j, to):
        return remote(mb.at[j], mb.at[j + 1], mr_send, mr_recv.at[j], to)

    def finish_meta(part, rows, far, high, unit):
        for k in range(SECTIONS):
            hops = mb[far[k]]
            for cc in range(2):
                line = hops[rows[cc] + k : rows[cc] + k + 1, :]
                lanes = lane[0:1, :]
                line = jnp.where(lanes == SLOTS, jnp.where(high[k], WIN, 0), line)
                line = jnp.where(lanes == SLOTS + 1, far[k] * unit, line)
                line = jnp.where(lanes == SLOTS + 2, lax.rem(NRING - far[k], NRING) * unit, line)
                line = jnp.where(lanes == SLOTS + 3, cc, line)
                line = jnp.where(lanes == SLOTS + 4, jnp.where(high[k], 1, 0), line)
                out = meta.at[part] if part == 1 - cc else mt
                out[k : k + 1, :] = line
        remote(mt, meta.at[part], mf_send, mf_recv, sibling).start()

    def b_copy(d, t):
        return remote(sb.at[d, t], rb.at[d, t], b_send.at[d], b_recv.at[d, t], z_to[d])

    def b_share(d, t):
        return remote(sb.at[d, t, 0], sb.at[d, t, 0], s_send.at[d], s_recv.at[d], sibling)

    @pl.when(core == 1)
    def _():
        greet(z_to + [sibling, yh_same, yh_cross])
        hand_over(xv, yh_same, 1, (0, 1, 2))
        sort()
        owner = [panels[k] // 2 for k in range(SECTIONS)]
        high = [lax.rem(panels[k], 2) == 1 for k in range(SECTIONS)]
        hand_meta(yh_same, 1).start()
        hand_meta(sibling, 0).start()
        hand_over(xa, sibling, 0)
        own_here = [owner[k] == row for k in range(SECTIONS)]
        own_there = [owner[k] == (1 - yh) * NZ + z for k in range(SECTIONS)]

        def b_round(t, i, q, first):
            rows = pl.ds(q * CB, CB)
            for d in range(2):
                slots = slots_of(i, d)
                if not first:
                    b_copy(d, t - MB).wait_recv()
                for cc in range(2):
                    if cc == 1:
                        here = [xv[s, rows, :] for s in slots]
                    else:
                        here = [pc[0, s, rows, :] for s in slots]
                    there = [pc[2 - cc, s, rows, :] for s in slots]
                    for k in range(SECTIONS):
                        v = here[0] if first else rb[d, t - MB, cc, k]
                        v = pick(high[k], there, own_there[k], v)
                        v = pick(high[k], here, own_here[k], v)
                        sb[d, t, cc, k] = v
                b_copy(d, t).start()
            for d in range(2):
                b_share(d, t).start()

        for i in range(HALF):
            handed(i + (i > 0), (0, 1, 2))
            hand_over(xv, yh_same, 1, ((3,), (5,), (6,))[i] if i < 3 else ())
            if i * QB < MB:
                for q in range(QB):
                    if i == 0 and q == FIRST // CB:
                        handed(1, (0, 1, 2))
                        hand_over(xv, yh_same, 1, (4,))
                    b_round(i * QB + q, i, q, i * QB + q < MB)
            else:
                def step(q, _, i=i):
                    b_round(i * QB + q, i, q, False)
                    return 0

                lax.fori_loop(0, QB, step, 0)
            if i == 0:
                for j in range(3):
                    hand_meta(sibling, j).wait_recv()
                for cc in range(2):
                    here = mo[0:1, :] if cc == 1 else mc[0, 0:1, :]
                    there = mc[2 - cc, 0:1, :]
                    for k in range(SECTIONS):
                        r = cc * SECTIONS + k
                        mb[0, r : r + 1, :] = jnp.where(own_here[k], here, there)
            else:
                ring_meta(i - 1, z_to[0]).wait_recv()
            ring_meta(i, z_to[0]).start()

        def tail(t, _):
            for d in range(2):
                b_copy(d, t - MB).wait_recv()
                sb[d, t] = rb[d, t - MB]

                @pl.when(t < TB_R)
                def _():
                    b_copy(d, t).start()

            for d in range(2):
                b_share(d, t).start()
            return 0

        lax.fori_loop(NB_R, NB_R + MB, tail, 0)
        ring_meta(HALF - 1, z_to[0]).wait_recv()
        ring_meta(HALF, z_to[0]).start()
        lax.fori_loop(NB_R + MB, NB_R + 5 * MB, tail, 0)
        ring_meta(HALF, z_to[0]).wait_recv()
        far = [lax.rem(z - lax.rem(owner[k], NZ) + NZ, NZ) for k in range(SECTIONS)]
        finish_meta(0, (0, SECTIONS), far, high, MB)
        lax.fori_loop(NB_R + 5 * MB, SB_R, tail, 0)
        for d in range(2):
            all_left(sb.at[d, pl.ds(0, TB_R)], b_send.at[d])
            all_left(sb.at[d, pl.ds(0, SB_R), 0], s_send.at[d])
            all_left(sa.at[d], s_recv.at[d])
        for j in (0, 1):
            all_left(pc.at[j], h_send.at[j])
            all_left(mo, mh_send.at[j])

    def a_copy(d, t):
        return remote(sa.at[d, t], ra.at[d, t], a_send.at[d], a_recv.at[d, t], x_to[d])

    def a_share(d, t):
        return remote(sa.at[d, t], sa.at[d, t], s_send.at[d], s_recv.at[d], sibling)

    @pl.when(core == 0)
    def _():
        greet(x_to + [sibling, yh_cross])
        hand_over(xv, yh_cross, 2, (0, 1, 2))
        hand_over(xv, sibling, 0)
        sort()
        owner = [panels[k] // 2 for k in range(SECTIONS)]
        high = [lax.rem(panels[k], 2) == 1 for k in range(SECTIONS)]
        hand_meta(yh_cross, 2).start()
        hand_meta(sibling, 0).start()
        own_here = [owner[k] == col for k in range(SECTIONS)]
        own_there = [owner[k] == col + 1 for k in range(SECTIONS)]

        def a_round(t, i, q, first):
            rows = pl.ds(q * CA, CA)
            for d in range(2):
                slots = slots_of(i, d)
                if not first:
                    a_copy(d, t - MA).wait_recv()
                here = [xa[s, rows, :] for s in slots]
                there = [pc[0, s, rows, :] for s in slots]
                for k in range(SECTIONS):
                    v = here[0] if first else ra[d, t - MA, k]
                    v = pick(high[k], there, own_there[k], v)
                    v = pick(high[k], here, own_here[k], v)
                    sa[d, t, k] = v
                a_copy(d, t).start()
            for d in range(2):
                a_share(d, t).start()

        for i in range(HALF):
            handed(i + (i > 0), (0,))
            hand_over(xv, yh_cross, 2, ((3,), (5,), (6,))[i] if i < 3 else ())
            if i * QA < MA:
                for q in range(QA):
                    if i == 0 and q == FIRST // CA:
                        handed(1, (0,))
                        hand_over(xv, yh_cross, 2, (4,))
                    a_round(i * QA + q, i, q, i * QA + q < MA)
            else:
                def step(q, _, i=i):
                    a_round(i * QA + q, i, q, False)
                    return 0

                lax.fori_loop(0, QA, step, 0)
            if i == 0:
                hand_meta(sibling, 0).wait_recv()
                for k in range(SECTIONS):
                    mb[0, k : k + 1, :] = jnp.where(own_here[k], mo[1:2, :], mc[0, 1:2, :])
                    mb[0, SECTIONS + k : SECTIONS + k + 1, :] = mo[0:1, :]
            else:
                ring_meta(i - 1, x_to[0]).wait_recv()
            ring_meta(i, x_to[0]).start()

        def tail(t, _):
            for d in range(2):
                a_copy(d, t - MA).wait_recv()
                sa[d, t] = ra[d, t - MA]

                @pl.when(t < TA_R)
                def _():
                    a_copy(d, t).start()

            for d in range(2):
                a_share(d, t).start()
            return 0

        lax.fori_loop(NA_R, NA_R + MA, tail, 0)
        ring_meta(HALF - 1, x_to[0]).wait_recv()
        ring_meta(HALF, x_to[0]).start()
        lax.fori_loop(NA_R + MA, NA_R + 5 * MA, tail, 0)
        ring_meta(HALF, x_to[0]).wait_recv()
        far = []
        for k in range(SECTIONS):
            xo, yo = lax.rem(owner[k] // 2, NX), owner[k] // 8
            far.append(lax.rem(place - jnp.where(yo == 0, xo, NRING - 1 - xo) + NRING, NRING))
        finish_meta(1, (0, 0), far, high, MA)
        lax.fori_loop(NA_R + 5 * MA, SA_R, tail, 0)
        for d in range(2):
            all_left(sa.at[d, pl.ds(0, TA_R)], a_send.at[d])
            all_left(sa.at[d], s_send.at[d])
            all_left(sb.at[d, pl.ds(0, SB_R), 0], s_recv.at[d])
        for j in (0, 2):
            all_left(pc.at[j], h_send.at[j])
            all_left(mo, mh_send.at[j])

    all_left(mb.at[pl.ds(0, NRING - 1)], mr_send)
    all_left(mt, mf_send)
    all_left(mt, mf_recv)


def product_kernel(meta, sb, sa, c_ref, a_full, b_full):
    @pl.when(pl.program_id(0) == 0)
    def _():
        a_full[...] = jnp.zeros_like(a_full)
        b_full[...] = jnp.zeros_like(b_full)

        def section(k, _):
            for part in range(2):
                late = meta[part, k, SLOTS]
                start = [meta[part, k, SLOTS + 1], meta[part, k, SLOTS + 2]]
                core = meta[part, k, SLOTS + 3]
                high = meta[part, k, SLOTS + 4]
                for w in range(WIN):
                    d = w // HALF
                    slots = slots_of(w % HALF, d)
                    p = meta[part, k, slots[0] + (late if len(slots) == 2 else 0)]
                    if part == 0:
                        @pl.when((p >> 5) == high)
                        def _(p=p, d=d, w=w, start=start, core=core):
                            v = sb[d, pl.ds(start[d] + (w % HALF) * QB, QB), core, k]
                            r0 = pl.multiple_of((k * PW + ((p >> 3) & 3)) * BS, BS)
                            c0 = pl.multiple_of((p & 7) * BS, BS)
                            b_full[pl.ds(r0, BS), pl.ds(c0, BS)] = v.reshape(BS, BS)
                    else:
                        @pl.when(((p >> 2) & 1) == high)
                        def _(p=p, d=d, w=w, start=start):
                            v = sa[d, pl.ds(start[d] + (w % HALF) * QA, QA), k]
                            r0 = pl.multiple_of((p >> 3) * BS, BS)
                            c0 = pl.multiple_of((k * PW + (p & 3)) * BS, BS)
                            a_full[pl.ds(r0, BS), pl.ds(c0, BS)] = v.reshape(BS, BS)
            return 0

        lax.fori_loop(0, SECTIONS, section, 0)

    rows = c_ref.shape[0]
    r0 = pl.multiple_of(pl.program_id(0) * rows, rows)
    c_ref[...] = jnp.dot(
        a_full[pl.ds(r0, rows), :], b_full[...], preferred_element_type=jnp.float32)


def per_device(x_tiles, tile_pos, panel_ids):
    vmem = pl.BlockSpec(memory_space=pltpu.VMEM)
    smem = pl.BlockSpec(memory_space=pltpu.SMEM)
    hbm = pl.BlockSpec(memory_space=pltpu.HBM)
    bf16, i32 = jnp.bfloat16, jnp.int32
    dma = pltpu.SemaphoreType.DMA
    sb, sa, meta = pl.pallas_call(
        comm_kernel,
        out_shape=[
            jax.ShapeDtypeStruct((2, SB_R, 2, SECTIONS, CB, BS), bf16),
            jax.ShapeDtypeStruct((2, SA_R, SECTIONS, CA, BS), bf16),
            jax.ShapeDtypeStruct((2, 8, BS), i32),
        ],
        in_specs=[hbm, hbm, hbm],
        out_specs=[vmem, vmem, vmem],
        scratch_shapes=[
            pltpu.SMEM((SECTIONS,), i32),
            pltpu.SMEM((1, SLOTS), i32),
            pltpu.VMEM((SLOTS, BS, BS), bf16),
            pltpu.VMEM((SLOTS, BS, BS), bf16),
            pltpu.VMEM((3, SLOTS, BS, BS), bf16),
            pltpu.VMEM((2, TB_R, 2, SECTIONS, CB, BS), bf16),
            pltpu.VMEM((2, TA_R, SECTIONS, CA, BS), bf16),
            pltpu.VMEM((8, BS), i32),
            pltpu.VMEM((3, 8, BS), i32),
            pltpu.VMEM((NRING, 8, BS), i32),
            pltpu.VMEM((8, BS), i32),
            dma, dma((2,)), dma((3,)), dma((3, len(PIECES))),
            dma((2,)), dma((2, TB_R)), dma((2,)), dma((2, TA_R)), dma((2,)), dma((2,)),
            dma((3,)), dma((3,)), dma, dma((NRING - 1,)), dma, dma,
        ],
        compiler_params=pltpu.CompilerParams(
            collective_id=0, has_side_effects=True, vmem_limit_bytes=28 << 20),
        name="spread_tiles",
    )(*[
        pltpu.with_memory_space_constraint(v, pltpu.HBM)
        for v in (panel_ids, tile_pos, x_tiles)
    ])
    n = LR * BS
    kdim = SECTIONS * PW * BS
    steps = 4
    return pl.pallas_call(
        product_kernel,
        out_shape=jax.ShapeDtypeStruct((n, LC * BS), jnp.float32),
        grid=(steps,),
        in_specs=[smem, vmem, vmem],
        out_specs=pl.BlockSpec((n // steps, LC * BS), lambda i: (i, 0)),
        scratch_shapes=[pltpu.VMEM((n, kdim), bf16), pltpu.VMEM((kdim, LC * BS), bf16)],
        compiler_params=pltpu.CompilerParams(vmem_limit_bytes=16 << 20),
        cost_estimate=pl.CostEstimate(
            flops=2 * n * kdim * LC * BS, bytes_accessed=10 << 20, transcendentals=0),
        name="panel_product",
    )(meta, sb, sa)


def solution(mesh):
    in_specs = (P("row", "col", None), P("row", "col"), P())
    out_specs = P("row", "col")
    return jax.shard_map(
        per_device, mesh=mesh, in_specs=in_specs, out_specs=out_specs, check_vma=False
    )
```

```python
import jax
import jax.numpy as jnp
from jax import lax
from jax.experimental import pallas as pl
from jax.experimental.pallas import tpu as pltpu
from jax.sharding import PartitionSpec as P

BS = 128
LR = 8
LC = 8
PW = 4
SECTIONS = 4
SLOTS = 16
WIN = 12
HALF = WIN // 2
LOW = SLOTS - WIN
NZ, NX = 8, 4
CB, CA = 16, 32
MB, MA = 7, 5
QB, QA = BS // CB, BS // CA
NB_R, NA_R = HALF * QB, HALF * QA
NRING = 8
TB_R, TA_R = NB_R + (NRING - 2) * MB, NA_R + (NRING - 2) * MA
SB_R, SA_R = TB_R + MB, TA_R + MA
MESH = pl.DeviceIdType.MESH

def slots_of(i, d):
    if i < (WIN - LOW) // 2:
        return [LOW + 2 * i + d]
    s = 2 * (i - (WIN - LOW) // 2) + d
    return [s, WIN + s]


FIRST = 32
HANDED = [
    [(s, 0, FIRST) for d in range(2) for s in slots_of(0, d)],
    [(s, FIRST, BS - FIRST) for d in range(2) for s in slots_of(0, d)],
]
for _i in range(1, HALF):
    HANDED.append([(s, 0, BS) for d in range(2) for s in slots_of(_i, d)])
PIECES = [piece for group in HANDED for piece in group]


def comm_kernel(
    panels_hbm, pos_hbm, x_hbm, sb, sa, meta,
    panels, pos, xv, xa, pc, rb, ra, mo, mc, mb, mt,
    x_sem, i_sem, h_send, h_recv, b_send, b_recv, a_send, a_recv, s_send, s_recv,
    mh_send, mh_recv, mr_send, mr_recv, mf_send, mf_recv,
):
    row = lax.axis_index("row")
    col = lax.axis_index("col")
    core = lax.rem(col, 2)
    z, yh = lax.rem(row, NZ), row // NZ
    x, yl = lax.rem(col // 2, NX), col // 8
    place = jnp.where(yl == 0, x, NRING - 1 - x)

    def dev(zz, yyh, xx, yyl, cc):
        return {"row": yyh * NZ + zz, "col": (yyl * NX + xx) * 2 + cc}

    def around(step):
        p = lax.rem(place + step, NRING)
        back = p // NX
        return dev(z, yh, jnp.where(back == 0, p, NRING - 1 - p), back, core)

    z_to = [dev(lax.rem(z + 1, NZ), yh, x, yl, core), dev(lax.rem(z + NZ - 1, NZ), yh, x, yl, core)]
    x_to = [around(1), around(NRING - 1)]
    sibling = dev(z, yh, x, yl, 1 - core)
    yh_same, yh_cross = dev(z, 1 - yh, x, yl, core), dev(z, 1 - yh, x, yl, 1 - core)

    def remote(src, dst, send, recv, to):
        return pltpu.make_async_remote_copy(
            src_ref=src, dst_ref=dst, send_sem=send, recv_sem=recv,
            device_id=to, device_id_type=MESH)

    fetch = [
        pltpu.make_async_copy(x_hbm, xv, x_sem),
        pltpu.make_async_copy(panels_hbm, panels, i_sem.at[0]),
        pltpu.make_async_copy(pos_hbm, pos, i_sem.at[1]),
    ]
    for f in fetch:
        f.start()
    barrier = pltpu.get_barrier_semaphore()

    def greet(peers):
        for peer in peers:
            pl.semaphore_signal(barrier, inc=1, device_id=peer, device_id_type=MESH)
        pl.semaphore_wait(barrier, len(peers))
        fetch[0].wait()

    lane = lax.broadcasted_iota(jnp.int32, (8, BS), 1)
    sub = lax.broadcasted_iota(jnp.int32, (8, BS), 0)

    def hand(source, to, j, n):
        s, r, rows = PIECES[n]
        at = (s, pl.ds(r, rows))
        return remote(
            source.at[at], pc.at[(j, *at)], h_send.at[j], h_recv.at[j, n], to)

    def hand_meta(to, j):
        return remote(mo, mc.at[j], mh_send.at[j], mh_recv.at[j], to)

    def hand_over(source, to, j, groups=range(len(HANDED))):
        for g in groups:
            for piece in HANDED[g]:
                hand(source, to, j, PIECES.index(piece)).start()

    def handed(g, js):
        for piece in HANDED[g]:
            for j in js:
                hand(xv, sibling, j, PIECES.index(piece)).wait_recv()

    def all_left(ref, sem):
        pltpu.make_async_copy(ref, ref, sem).wait()

    def pick(own, low_high, cond, v):
        mine = low_high[0]
        if len(low_high) == 2:
            mine = lax.select(own, low_high[1], mine)
        return lax.select(cond, mine, v)

    def sort():
        fetch[1].wait()
        fetch[2].wait()
        spot = [pos[0, s] for s in range(SLOTS)]
        right = [lax.rem(p, LC) // PW for p in spot]
        lefts, rights, rank = 0, SLOTS - sum(right), []
        for s in range(SLOTS):
            rank.append(jnp.where(right[s] == 0, lefts, rights))
            lefts, rights = lefts + 1 - right[s], rights + right[s]
        where = jnp.zeros((8, BS), jnp.int32)
        for s in range(SLOTS):
            where = jnp.where((sub == 0) & (lane == s), spot[s], where)
            where = jnp.where((sub == 1) & (lane == rank[s]), spot[s], where)
        mo[...] = where
        for i in range(SLOTS):
            src = sum(jnp.where(rank[s] == i, s, 0) for s in range(SLOTS))
            xa[i] = xv[src]

    def ring_meta(j, to):
        return remote(mb.at[j], mb.at[j + 1], mr_send, mr_recv.at[j], to)

    def finish_meta(part, rows, far, high, unit):
        for k in range(SECTIONS):
            hops = mb[far[k]]
            for cc in range(2):
                line = hops[rows[cc] + k : rows[cc] + k + 1, :]
                lanes = lane[0:1, :]
                line = jnp.where(lanes == SLOTS, jnp.where(high[k], WIN, 0), line)
                line = jnp.where(lanes == SLOTS + 1, far[k] * unit, line)
                line = jnp.where(lanes == SLOTS + 2, lax.rem(NRING - far[k], NRING) * unit, line)
                line = jnp.where(lanes == SLOTS + 3, cc, line)
                line = jnp.where(lanes == SLOTS + 4, jnp.where(high[k], 1, 0), line)
                out = meta.at[part] if part == 1 - cc else mt
                out[k : k + 1, :] = line
        remote(mt, meta.at[part], mf_send, mf_recv, sibling).start()

    def b_copy(d, t):
        return remote(sb.at[d, t], rb.at[d, t], b_send.at[d], b_recv.at[d, t], z_to[d])

    def b_share(d, t):
        return remote(sb.at[d, t, 0], sb.at[d, t, 0], s_send.at[d], s_recv.at[d], sibling)

    @pl.when(core == 1)
    def _():
        greet(z_to + [sibling, yh_same, yh_cross])
        hand_over(xv, yh_same, 1, (0, 1, 2))
        sort()
        owner = [panels[k] // 2 for k in range(SECTIONS)]
        high = [lax.rem(panels[k], 2) == 1 for k in range(SECTIONS)]
        hand_meta(yh_same, 1).start()
        hand_meta(sibling, 0).start()
        hand_over(xa, sibling, 0)
        own_here = [owner[k] == row for k in range(SECTIONS)]
        own_there = [owner[k] == (1 - yh) * NZ + z for k in range(SECTIONS)]

        def b_round(t, i, q, first):
            rows = pl.ds(q * CB, CB)
            for d in range(2):
                slots = slots_of(i, d)
                if not first:
                    b_copy(d, t - MB).wait_recv()
                for cc in range(2):
                    if cc == 1:
                        here = [xv[s, rows, :] for s in slots]
                    else:
                        here = [pc[0, s, rows, :] for s in slots]
                    there = [pc[2 - cc, s, rows, :] for s in slots]
                    for k in range(SECTIONS):
                        v = here[0] if first else rb[d, t - MB, cc, k]
                        v = pick(high[k], there, own_there[k], v)
                        v = pick(high[k], here, own_here[k], v)
                        sb[d, t, cc, k] = v
                b_copy(d, t).start()
            for d in range(2):
                b_share(d, t).start()

        for i in range(HALF):
            handed(i + (i > 0), (0, 1, 2))
            hand_over(xv, yh_same, 1, ((3,), (5,), (6,))[i] if i < 3 else ())
            if i * QB < MB:
                for q in range(QB):
                    if i == 0 and q == FIRST // CB:
                        handed(1, (0, 1, 2))
                        hand_over(xv, yh_same, 1, (4,))
                    b_round(i * QB + q, i, q, i * QB + q < MB)
            else:
                def step(q, _, i=i):
                    b_round(i * QB + q, i, q, False)
                    return 0

                lax.fori_loop(0, QB, step, 0)
            if i == 0:
                for j in range(3):
                    hand_meta(sibling, j).wait_recv()
                for cc in range(2):
                    here = mo[0:1, :] if cc == 1 else mc[0, 0:1, :]
                    there = mc[2 - cc, 0:1, :]
                    for k in range(SECTIONS):
                        r = cc * SECTIONS + k
                        mb[0, r : r + 1, :] = jnp.where(own_here[k], here, there)
            else:
                ring_meta(i - 1, z_to[0]).wait_recv()
            ring_meta(i, z_to[0]).start()

        def tail(t, _):
            for d in range(2):
                b_copy(d, t - MB).wait_recv()

                @pl.when(t < TB_R)
                def _():
                    remote(rb.at[d, t - MB], rb.at[d, t], b_send.at[d], b_recv.at[d, t], z_to[d]).start()

                sb[d, t] = rb[d, t - MB]

            for d in range(2):
                b_share(d, t).start()
            return 0

        lax.fori_loop(NB_R, NB_R + MB, tail, 0)
        ring_meta(HALF - 1, z_to[0]).wait_recv()
        ring_meta(HALF, z_to[0]).start()
        lax.fori_loop(NB_R + MB, NB_R + 5 * MB, tail, 0)
        ring_meta(HALF, z_to[0]).wait_recv()
        far = [lax.rem(z - lax.rem(owner[k], NZ) + NZ, NZ) for k in range(SECTIONS)]
        finish_meta(0, (0, SECTIONS), far, high, MB)
        lax.fori_loop(NB_R + 5 * MB, SB_R, tail, 0)
        for d in range(2):
            all_left(sb.at[d, pl.ds(0, TB_R)], b_send.at[d])
            all_left(sb.at[d, pl.ds(0, SB_R), 0], s_send.at[d])
            all_left(sa.at[d], s_recv.at[d])
        for j in (0, 1):
            all_left(pc.at[j], h_send.at[j])
            all_left(mo, mh_send.at[j])

    def a_copy(d, t):
        return remote(sa.at[d, t], ra.at[d, t], a_send.at[d], a_recv.at[d, t], x_to[d])

    def a_share(d, t):
        return remote(sa.at[d, t], sa.at[d, t], s_send.at[d], s_recv.at[d], sibling)

    @pl.when(core == 0)
    def _():
        greet(x_to + [sibling, yh_cross])
        hand_over(xv, yh_cross, 2, (0, 1, 2))
        hand_over(xv, sibling, 0)
        sort()
        owner = [panels[k] // 2 for k in range(SECTIONS)]
        high = [lax.rem(panels[k], 2) == 1 for k in range(SECTIONS)]
        hand_meta(yh_cross, 2).start()
        hand_meta(sibling, 0).start()
        own_here = [owner[k] == col for k in range(SECTIONS)]
        own_there = [owner[k] == col + 1 for k in range(SECTIONS)]

        def a_round(t, i, q, first):
            rows = pl.ds(q * CA, CA)
            for d in range(2):
                slots = slots_of(i, d)
                if not first:
                    a_copy(d, t - MA).wait_recv()
                here = [xa[s, rows, :] for s in slots]
                there = [pc[0, s, rows, :] for s in slots]
                for k in range(SECTIONS):
                    v = here[0] if first else ra[d, t - MA, k]
                    v = pick(high[k], there, own_there[k], v)
                    v = pick(high[k], here, own_here[k], v)
                    sa[d, t, k] = v
                a_copy(d, t).start()
            for d in range(2):
                a_share(d, t).start()

        for i in range(HALF):
            handed(i + (i > 0), (0,))
            hand_over(xv, yh_cross, 2, ((3,), (5,), (6,))[i] if i < 3 else ())
            if i * QA < MA:
                for q in range(QA):
                    if i == 0 and q == FIRST // CA:
                        handed(1, (0,))
                        hand_over(xv, yh_cross, 2, (4,))
                    a_round(i * QA + q, i, q, i * QA + q < MA)
            else:
                def step(q, _, i=i):
                    a_round(i * QA + q, i, q, False)
                    return 0

                lax.fori_loop(0, QA, step, 0)
            if i == 0:
                hand_meta(sibling, 0).wait_recv()
                for k in range(SECTIONS):
                    mb[0, k : k + 1, :] = jnp.where(own_here[k], mo[1:2, :], mc[0, 1:2, :])
                    mb[0, SECTIONS + k : SECTIONS + k + 1, :] = mo[0:1, :]
            else:
                ring_meta(i - 1, x_to[0]).wait_recv()
            ring_meta(i, x_to[0]).start()

        def tail(t, _):
            for d in range(2):
                a_copy(d, t - MA).wait_recv()

                @pl.when(t < TA_R)
                def _():
                    remote(ra.at[d, t - MA], ra.at[d, t], a_send.at[d], a_recv.at[d, t], x_to[d]).start()

                sa[d, t] = ra[d, t - MA]

            for d in range(2):
                a_share(d, t).start()
            return 0

        lax.fori_loop(NA_R, NA_R + MA, tail, 0)
        ring_meta(HALF - 1, x_to[0]).wait_recv()
        ring_meta(HALF, x_to[0]).start()
        lax.fori_loop(NA_R + MA, NA_R + 5 * MA, tail, 0)
        ring_meta(HALF, x_to[0]).wait_recv()
        far = []
        for k in range(SECTIONS):
            xo, yo = lax.rem(owner[k] // 2, NX), owner[k] // 8
            far.append(lax.rem(place - jnp.where(yo == 0, xo, NRING - 1 - xo) + NRING, NRING))
        finish_meta(1, (0, 0), far, high, MA)
        lax.fori_loop(NA_R + 5 * MA, SA_R, tail, 0)
        for d in range(2):
            all_left(sa.at[d, pl.ds(0, TA_R)], a_send.at[d])
            all_left(sa.at[d], s_send.at[d])
            all_left(sb.at[d, pl.ds(0, SB_R), 0], s_recv.at[d])
        for j in (0, 2):
            all_left(pc.at[j], h_send.at[j])
            all_left(mo, mh_send.at[j])

    all_left(mb.at[pl.ds(0, NRING - 1)], mr_send)
    all_left(mt, mf_send)
    all_left(mt, mf_recv)


def product_kernel(meta, sb, sa, c_ref, a_full, b_full):
    @pl.when(pl.program_id(0) == 0)
    def _():
        a_full[...] = jnp.zeros_like(a_full)
        b_full[...] = jnp.zeros_like(b_full)

        def section(k, _):
            for part in range(2):
                late = meta[part, k, SLOTS]
                start = [meta[part, k, SLOTS + 1], meta[part, k, SLOTS + 2]]
                core = meta[part, k, SLOTS + 3]
                high = meta[part, k, SLOTS + 4]
                for w in range(WIN):
                    d = w // HALF
                    slots = slots_of(w % HALF, d)
                    p = meta[part, k, slots[0] + (late if len(slots) == 2 else 0)]
                    if part == 0:
                        @pl.when((p >> 5) == high)
                        def _(p=p, d=d, w=w, start=start, core=core):
                            v = sb[d, pl.ds(start[d] + (w % HALF) * QB, QB), core, k]
                            r0 = pl.multiple_of((k * PW + ((p >> 3) & 3)) * BS, BS)
                            c0 = pl.multiple_of((p & 7) * BS, BS)
                            b_full[pl.ds(r0, BS), pl.ds(c0, BS)] = v.reshape(BS, BS)
                    else:
                        @pl.when(((p >> 2) & 1) == high)
                        def _(p=p, d=d, w=w, start=start):
                            v = sa[d, pl.ds(start[d] + (w % HALF) * QA, QA), k]
                            r0 = pl.multiple_of((p >> 3) * BS, BS)
                            c0 = pl.multiple_of((k * PW + (p & 3)) * BS, BS)
                            a_full[pl.ds(r0, BS), pl.ds(c0, BS)] = v.reshape(BS, BS)
            return 0

        lax.fori_loop(0, SECTIONS, section, 0)

    rows = c_ref.shape[0]
    r0 = pl.multiple_of(pl.program_id(0) * rows, rows)
    c_ref[...] = jnp.dot(
        a_full[pl.ds(r0, rows), :], b_full[...], preferred_element_type=jnp.float32)


def per_device(x_tiles, tile_pos, panel_ids):
    vmem = pl.BlockSpec(memory_space=pltpu.VMEM)
    smem = pl.BlockSpec(memory_space=pltpu.SMEM)
    hbm = pl.BlockSpec(memory_space=pltpu.HBM)
    bf16, i32 = jnp.bfloat16, jnp.int32
    dma = pltpu.SemaphoreType.DMA
    sb, sa, meta = pl.pallas_call(
        comm_kernel,
        out_shape=[
            jax.ShapeDtypeStruct((2, SB_R, 2, SECTIONS, CB, BS), bf16),
            jax.ShapeDtypeStruct((2, SA_R, SECTIONS, CA, BS), bf16),
            jax.ShapeDtypeStruct((2, 8, BS), i32),
        ],
        in_specs=[hbm, hbm, hbm],
        out_specs=[vmem, vmem, vmem],
        scratch_shapes=[
            pltpu.SMEM((SECTIONS,), i32),
            pltpu.SMEM((1, SLOTS), i32),
            pltpu.VMEM((SLOTS, BS, BS), bf16),
            pltpu.VMEM((SLOTS, BS, BS), bf16),
            pltpu.VMEM((3, SLOTS, BS, BS), bf16),
            pltpu.VMEM((2, TB_R, 2, SECTIONS, CB, BS), bf16),
            pltpu.VMEM((2, TA_R, SECTIONS, CA, BS), bf16),
            pltpu.VMEM((8, BS), i32),
            pltpu.VMEM((3, 8, BS), i32),
            pltpu.VMEM((NRING, 8, BS), i32),
            pltpu.VMEM((8, BS), i32),
            dma, dma((2,)), dma((3,)), dma((3, len(PIECES))),
            dma((2,)), dma((2, TB_R)), dma((2,)), dma((2, TA_R)), dma((2,)), dma((2,)),
            dma((3,)), dma((3,)), dma, dma((NRING - 1,)), dma, dma,
        ],
        compiler_params=pltpu.CompilerParams(
            collective_id=0, has_side_effects=True, vmem_limit_bytes=28 << 20),
        name="spread_tiles",
    )(*[
        pltpu.with_memory_space_constraint(v, pltpu.HBM)
        for v in (panel_ids, tile_pos, x_tiles)
    ])
    n = LR * BS
    kdim = SECTIONS * PW * BS
    steps = 4
    return pl.pallas_call(
        product_kernel,
        out_shape=jax.ShapeDtypeStruct((n, LC * BS), jnp.float32),
        grid=(steps,),
        in_specs=[smem, vmem, vmem],
        out_specs=pl.BlockSpec((n // steps, LC * BS), lambda i: (i, 0)),
        scratch_shapes=[pltpu.VMEM((n, kdim), bf16), pltpu.VMEM((kdim, LC * BS), bf16)],
        compiler_params=pltpu.CompilerParams(vmem_limit_bytes=16 << 20),
        cost_estimate=pl.CostEstimate(
            flops=2 * n * kdim * LC * BS, bytes_accessed=10 << 20, transcendentals=0),
        name="panel_product",
    )(meta, sb, sa)


def solution(mesh):
    in_specs = (P("row", "col", None), P("row", "col"), P())
    out_specs = P("row", "col")
    return jax.shard_map(
        per_device, mesh=mesh, in_specs=in_specs, out_specs=out_specs, check_vma=False
    )
```
